128 devices in a mesh: row: 16 (over x, z), col: 8 (over y, core).
Axes of the slice: x: 4, y: 4, z: 4, core: 2. Of those that a mesh axis runs over, the one named last changes fastest.
Arguments:
- a_blocks: float32 [4096, 6, 4096], P(('row', 'col')), as said below
- columns: int32 [4096, 6], P(('row', 'col')), may hold values from 0 to 4095, as said below
- tentative: float32 [4096, 4096], P(('row', 'col')), may hold values from -0.75 to 0.75
- aggregate: int32 [4096], P(('row', 'col')), may hold values from 0 to 3, as said below
- owner: int32 [512], P(('row', 'col')), may hold values from 0 to 511, as said below
Outputs:
- coarse_op: float32 [512, 20, 4096], P(('row', 'col'))
The draws below stay inside these ranges and needn't reach their ends.
Inputs may be any that keep to these rules, and one draw needn't show every extreme that they name: Column 0 of block row n is n. Other columns of block row n lie among the block rows of n's device (32 a device, devices in the order of row+col); for the first 8 rows of a device they may also lie among the last 8 rows of the device before it, and for the last 8 rows among the first 8 rows of the device after it, and each such rim row of a device with that neighbour has one. Columns may repeat; repeated blocks add. `aggregate`: every device uses every number from 0 to 3. `owner`: A permutation of the coarse rows. The coarse rows of a device (a // 4) go to positions owned (position // 4) by devices of the same index along row, at most one to each device, so each device owns 4. The diagonal entries of the blocks a_blocks[n, 0] lie between 1.5 and 8.5.
All inputs are finite; a program needn't handle non-finite values.
Results may differ from the reference program's by a relative error of at most 0.0003.
Values sent between devices are 32-bit elements; how exact they have to be, the bound alone decides.
A program may use at most 256 MiB of HBM per device.

```python
import math
import jax
import jax.numpy as jnp
from jax import lax

B = 64
BC = 64
K = 6
G = 4
R = 32
H = 8
NBLK = 4096
NAGG = 512
N_COL = 8


def draw_a_blocks(key, part):
    key_off, key_diag = jax.random.split(key)
    offdiag = jnp.clip(jax.random.normal(key_off, (NBLK, K, B * B), jnp.float32), -4.0, 4.0) / B ** 0.5
    diag_values = jnp.exp(jax.random.uniform(key_diag, (NBLK, B), jnp.float32, math.log(2.0), math.log(8.0)))
    identity = (jnp.arange(B)[:, None] == jnp.arange(B)[None, :]).astype(jnp.float32)
    self_block = (diag_values[:, :, None] * identity[None]).reshape(NBLK, B * B)
    first_column = (jnp.arange(K) == 0).astype(jnp.float32)
    return offdiag + first_column[None, :, None] * self_block[:, None, :]


def draw_columns(key, part):
    key_own, key_low, key_up, key_coin = jax.random.split(key, 4)
    row_ids = jnp.arange(NBLK, dtype=jnp.int32)
    owner_dev = row_ids // R
    position = row_ids % R
    device_count = NBLK // R
    own_cols = owner_dev[:, None] * R + jax.random.randint(key_own, (NBLK, K), 0, R)
    lower_cols = (owner_dev[:, None] - 1) * R + R - H + jax.random.randint(key_low, (NBLK, K), 0, H)
    upper_cols = (owner_dev[:, None] + 1) * R + jax.random.randint(key_up, (NBLK, K), 0, H)
    coin_flip = jax.random.randint(key_coin, (NBLK, K), 0, 2)
    coin_flip = jnp.where(jnp.arange(K)[None, :] == 1, 1, coin_flip)
    use_lower = (position[:, None] < H) & (owner_dev[:, None] > 0) & (coin_flip == 1)
    use_upper = (position[:, None] >= R - H) & (owner_dev[:, None] < device_count - 1) & (coin_flip == 1)
    chosen = jnp.where(use_lower, lower_cols, jnp.where(use_upper, upper_cols, own_cols))
    chosen = jnp.where(jnp.arange(K)[None, :] == 0, row_ids[:, None], chosen)
    return chosen.astype(jnp.int32)


def draw_aggregate(key, part):
    key_perm, key_base = jax.random.split(key)
    device_count = NBLK // R
    orders = jax.vmap(lambda subkey: jax.random.permutation(subkey, R))(jax.random.split(key_perm, device_count))
    base_ids = jax.random.randint(key_base, (device_count, R), 0, G)
    chosen = jnp.where(orders < G, orders, base_ids)
    return chosen.reshape(NBLK).astype(jnp.int32)


def draw_owner(key, part):
    group_count = NAGG // (G * N_COL)
    shifts = jax.vmap(lambda subkey: jax.random.permutation(subkey, N_COL)[:G])(jax.random.split(key, group_count))
    coarse_ids = jnp.arange(NAGG, dtype=jnp.int32)
    anchor = coarse_ids // G
    within = coarse_ids % G
    group_ids = anchor // N_COL
    column_ids = anchor % N_COL
    moved = shifts[group_ids, within]
    return (group_ids * N_COL * G + (column_ids + moved) % N_COL * G + within).astype(jnp.int32)


def shard_levels(key, extent, cuts, smallest, largest):
    def one(dim, shards_of):
        steps = jax.random.uniform(jax.random.fold_in(jax.random.fold_in(key, 6), dim), (shards_of,), jnp.float32, smallest / len(cuts), largest / len(cuts))
        return jnp.repeat(jnp.exp(steps), extent[dim] // shards_of).reshape((-1,) + (1,) * (len(extent) - dim - 1))

    gain = one(*cuts[0])
    for cut in cuts[1:]:
        gain = gain * one(*cut)
    return gain


def gaussian(stream_key, dims, scale, most, shards=(), kind=jnp.bfloat16):
    array = jax.random.normal(stream_key, dims, jnp.float32) * scale
    if len(shards) > 0:
        array = shard_levels(stream_key, dims, shards, -0.22, 0.18) * array
    return jnp.clip(array, min=-most, max=most).astype(kind)


def setup_inputs(seed: int = 0) -> dict:
    key_list = jax.random.split(jax.random.key(seed), 6)
    return {
        "a_blocks": draw_a_blocks(jax.random.fold_in(key_list[5], 71), 0),
        "columns": draw_columns(jax.random.fold_in(key_list[5], 71), 0),
        "tentative": gaussian(key_list[2], (NBLK, B * BC), B ** -0.5, 0.75, ((0, 128),), jnp.float32),
        "aggregate": draw_aggregate(jax.random.fold_in(key_list[5], 71), 0),
        "owner": draw_owner(jax.random.fold_in(key_list[5], 71), 0),
    }


highest = lax.Precision.HIGHEST
relaxation = 2.0 / 3.0


def prolong_rows(a_rows, col_rows, own_basis, ext_basis, ext_agg, device):
    row_count = col_rows.shape[0]
    local_index = (col_rows - device * R + H).astype(jnp.int32)
    dev_offset = (local_index >= H).astype(jnp.int32) + (local_index >= R + H).astype(jnp.int32)
    labels = (dev_offset * G + jnp.take(ext_agg, local_index)).astype(jnp.int32)
    a_mats = a_rows.reshape(row_count, K, B, B)
    basis_rows = jnp.take(ext_basis, local_index, axis=0).reshape(row_count, K, B, BC)
    applied = jnp.einsum("ikqp,ikpv->ikqv", a_mats, basis_rows, precision=highest)
    diagonal = jnp.diagonal(a_mats[:, 0], axis1=1, axis2=2)
    first_column = (jnp.arange(K) == 0).astype(applied.dtype)
    smooth = first_column[None, :, None, None] * own_basis.reshape(row_count, 1, B, BC) - relaxation * applied / diagonal[:, None, :, None]
    return smooth.reshape(row_count, K, B * BC), labels


def apply_rows(a_group, index_group, ext_smooth, ext_labels):
    count = index_group.shape[0]
    gathered = jnp.take(ext_smooth, index_group, axis=0).reshape(count, K, K, B, BC)
    near_labels = jnp.take(ext_labels, index_group, axis=0)
    onehot = (near_labels[..., None] == jnp.arange(3 * G, dtype=jnp.int32)).astype(gathered.dtype)
    products = jnp.einsum("skqp,skmpw->skmqw", a_group.reshape(count, K, B, B), gathered, precision=highest)
    return jnp.einsum("skmc,skmqw->scqw", onehot, products, precision=highest)


def coarse_part(smooth, labels, applied_rows):
    count = labels.shape[0]
    onehot = (labels[..., None] == jnp.arange(3 * G, dtype=jnp.int32)).astype(smooth.dtype)
    dense = jnp.einsum("ikl,ikqv->ilqv", onehot, smooth.reshape(count, K, B, BC), precision=highest)
    return jnp.einsum("ilqv,icqw->lcvw", dense, applied_rows, precision=highest)


def reference(a_blocks, columns, tentative, aggregate, owner):
    device_count = NBLK // R
    pad_basis = jnp.pad(tentative, ((H, H), (0, 0)))
    pad_agg = jnp.pad(aggregate, (H, H))
    devices = jnp.arange(device_count, dtype=jnp.int32)

    def prolong(device):
        start_row = device * R
        ext_basis = lax.dynamic_slice_in_dim(pad_basis, start_row, R + 2 * H, 0)
        ext_agg = lax.dynamic_slice_in_dim(pad_agg, start_row, R + 2 * H, 0)
        a_rows = lax.dynamic_slice_in_dim(a_blocks, start_row, R, 0)
        col_rows = lax.dynamic_slice_in_dim(columns, start_row, R, 0)
        own_basis = lax.dynamic_slice_in_dim(tentative, start_row, R, 0)
        return prolong_rows(a_rows, col_rows, own_basis, ext_basis, ext_agg, device)

    smooth_all, labels_all = lax.map(prolong, devices)
    smooth_pad = jnp.pad(smooth_all, ((1, 1), (0, 0), (0, 0), (0, 0)))
    labels_pad = jnp.pad(labels_all, ((1, 1), (0, 0), (0, 0)))

    def assemble(device):
        start_row = device * R
        own_rows = lax.dynamic_index_in_dim(smooth_all, device, 0, False)
        own_labels = lax.dynamic_index_in_dim(labels_all, device, 0, False)
        lower_rows = lax.dynamic_index_in_dim(smooth_pad, device, 0, False)[R - H:]
        upper_rows = lax.dynamic_index_in_dim(smooth_pad, device + 2, 0, False)[:H]
        lower_labels = lax.dynamic_index_in_dim(labels_pad, device, 0, False)[R - H:] - G
        upper_labels = lax.dynamic_index_in_dim(labels_pad, device + 2, 0, False)[:H] + G
        ext_smooth = jnp.concatenate([lower_rows, own_rows, upper_rows], axis=0)
        ext_labels = jnp.concatenate([lower_labels, own_labels, upper_labels], axis=0).astype(jnp.int32)
        a_rows = lax.dynamic_slice_in_dim(a_blocks, start_row, R, 0)
        col_rows = lax.dynamic_slice_in_dim(columns, start_row, R, 0)
        local_index = (col_rows - start_row + H).astype(jnp.int32)
        applied_rows = apply_rows(a_rows, local_index, ext_smooth, ext_labels)
        return coarse_part(own_rows, own_labels, applied_rows)

    parts = lax.map(assemble, devices)
    parts_pad = jnp.pad(parts, ((1, 1), (0, 0), (0, 0), (0, 0), (0, 0)))
    own_part = parts[:, G:2 * G]
    from_lower = parts_pad[:-2, 2 * G:]
    from_upper = parts_pad[2:, :G]
    rows_full = jnp.pad(own_part, ((0, 0), (0, 0), (G, G), (0, 0), (0, 0)))
    rows_full = rows_full + jnp.pad(from_lower, ((0, 0), (0, 0), (0, 2 * G), (0, 0), (0, 0)))
    rows_full = rows_full + jnp.pad(from_upper, ((0, 0), (0, 0), (2 * G, 0), (0, 0), (0, 0)))
    coarse_rows = rows_full.reshape(NAGG, 5 * G, BC * BC)
    return jnp.zeros_like(coarse_rows).at[owner].set(coarse_rows)
```

```python
import functools

import jax
import jax.numpy as jnp
from jax import lax
from jax.experimental import pallas as pl
from jax.experimental.pallas import tpu as pltpu
from jax.sharding import PartitionSpec as P

B = 64
K = 6
G = 4
R = 32
H = 8
BB = B * B
GW = G * B
LANES = 128
relaxation = 2.0 / 3.0
f32 = jnp.float32
bf16 = jnp.bfloat16


def lane_low(rows):
    return lax.broadcasted_iota(jnp.int32, (rows, LANES), 1) < B


def natural_dup(half_rows, scratch):
    low = lane_low(B // 2)
    swapped = pltpu.roll(half_rows, B, 1)
    scratch[pl.ds(0, B // 2, stride=2), :] = jnp.where(low, half_rows, swapped)
    scratch[pl.ds(1, B // 2, stride=2), :] = jnp.where(low, swapped, half_rows)


def smooth_kernel(cols, aggs, a_ref, t_low, t_own, t_high, p_ref, aa_ref, flat, nat, t_nat, t_split):
    step = pl.program_id(0)
    rows = a_ref.shape[0]
    low = lane_low(B)

    @pl.when(step == 0)
    def _():
        for chunk in range(R // 8 + 2):
            source = t_low if chunk == 0 else t_high if chunk == R // 8 + 1 else t_own
            first = 0 if chunk in (0, R // 8 + 1) else (chunk - 1) * 8
            for c in range(B // 2):
                flat[pl.ds(c * 8, 8), :] = source[first : first + 8, c * LANES : (c + 1) * LANES]

            def one(j, carry):
                n = chunk * 8 + j
                natural_dup(flat[pl.ds(j, B // 2, stride=8), :], t_nat.at[n])
                value = t_nat[n]
                high = value.astype(bf16)
                t_split[n, 0:B, :] = high
                t_split[n, B : 2 * B, :] = (value - high.astype(f32)).astype(bf16)
                return carry

            lax.fori_loop(0, 8, one, 0)

    sub = lax.broadcasted_iota(jnp.int32, (B, LANES), 0)
    lane = lax.broadcasted_iota(jnp.int32, (B, LANES), 1)
    on_diagonal = sub == lane

    for r in range(rows):
        n = step * rows + r
        for c in range(B // 2):
            flat[pl.ds(c * 8, K), :] = a_ref[r, :, c * LANES : (c + 1) * LANES]
        for part in range(4):
            p_ref[r, :, part * LANES : (part + 1) * LANES] = jnp.zeros((B, LANES), f32)
        scale = None
        for k in range(K):
            ci = cols[n * K + k]
            natural_dup(flat[pl.ds(k, B // 2, stride=8), :], nat.at[k % 2])
            value = nat[k % 2]
            if k == 0:
                diagonal = jnp.sum(jnp.where(on_diagonal, value, 0.0), axis=1, keepdims=True)
                scale = relaxation / diagonal
            high = value.astype(bf16).astype(f32)
            pieces = jnp.where(low, high, value - high).astype(bf16)
            aa_ref[r, k] = pieces
            basis = t_split[ci]
            weights = jnp.concatenate([basis[:B], basis[:B], basis[B:], basis[B:]], axis=0)
            applied = jnp.dot(
                jnp.concatenate([pieces, pieces], axis=1), weights, preferred_element_type=f32
            )
            smooth = -applied * scale
            if k == 0:
                smooth = smooth + t_nat[n + H]
            label = aggs[ci]
            outside = jnp.logical_or(ci < H, ci >= R + H).astype(jnp.int32)
            place = pl.multiple_of((outside * 2 + label // 2) * LANES, LANES)
            keep = jnp.where(low, 1 - label % 2, label % 2) == 1
            window = (r, slice(None), pl.ds(place, LANES))
            p_ref[window] = p_ref[window] + jnp.where(keep, smooth, 0.0)


def smooth_rows(a_blocks, t_low, t_own, t_high, cols, aggs):
    rows = 4
    whole = lambda shape: pl.BlockSpec(shape, lambda i, *_: (0,) * len(shape))
    return pl.pallas_call(
        smooth_kernel,
        out_shape=(
            jax.ShapeDtypeStruct((R, B, 2 * GW), f32),
            jax.ShapeDtypeStruct((R, K, B, LANES), bf16),
        ),
        grid_spec=pltpu.PrefetchScalarGridSpec(
            num_scalar_prefetch=2,
            grid=(R // rows,),
            in_specs=[
                pl.BlockSpec((rows, K, BB), lambda i, *_: (i, 0, 0)),
                whole((H, BB)),
                whole((R, BB)),
                whole((H, BB)),
            ],
            out_specs=(
                pl.BlockSpec((rows, B, 2 * GW), lambda i, *_: (i, 0, 0)),
                pl.BlockSpec((rows, K, B, LANES), lambda i, *_: (i, 0, 0, 0)),
            ),
            scratch_shapes=[
                pltpu.VMEM((B // 2 * 8, LANES), f32),
                pltpu.VMEM((2, B, LANES), f32),
                pltpu.VMEM((R + 2 * H, B, LANES), f32),
                pltpu.VMEM((R + 2 * H, 2 * B, LANES), bf16),
            ],
        ),
        compiler_params=pltpu.CompilerParams(vmem_limit_bytes=40 << 20),
        name="smooth",
    )(cols, aggs, a_blocks, t_low, t_own, t_high)


def coarse_kernel(cols, aa_ref, p_own, p_low, p_high, out_ref, p_split, ap):
    step = pl.program_id(0)
    rows = aa_ref.shape[0]

    def split(value):
        high = value.astype(bf16)
        return high, (value - high.astype(f32)).astype(bf16)

    @pl.when(step == 0)
    def _():
        out_ref[...] = jnp.zeros_like(out_ref)

        def own(n, carry):
            high, low = split(p_own[n])
            p_split[n + H, 0:B, :] = high
            p_split[n + H, B : 2 * B, :] = low
            return carry

        lax.fori_loop(0, R, own, 0)
        for source, base in ((p_low, 0), (p_high, R + H)):

            def halo(n, carry, source=source, base=base):
                for half in range(2):
                    high, low = split(source[n, :, (1 - half) * GW : (2 - half) * GW])
                    p_split[base + n, 0:B, half * GW : (half + 1) * GW] = high
                    p_split[base + n, B : 2 * B, half * GW : (half + 1) * GW] = low
                return carry

            lax.fori_loop(0, H, halo, 0)

    ap[0] = jnp.zeros_like(ap[0])
    ap[2] = jnp.zeros_like(ap[2])
    for r in range(rows):
        n = step * rows + r
        total = jnp.zeros((B, GW), f32)
        for k in range(K):
            ci = cols[n * K + k]
            pieces = aa_ref[r, k]
            basis = p_split[ci]
            weights = jnp.concatenate([basis[:B], basis[:B], basis[B:], basis[B:]], axis=0)
            applied = jnp.dot(
                jnp.concatenate([pieces, pieces], axis=1), weights, preferred_element_type=f32
            )
            total = total + applied[:, :GW]
            window = (jnp.where(ci < R // 2, 0, 2), slice(r * B, (r + 1) * B), slice(None))
            ap[window] = ap[window] + applied[:, GW:]
        ap[1, r * B : (r + 1) * B, :] = total

    def product(left, right):
        return lax.dot_general(left, right, (((0,), (0,)), ((), ())), preferred_element_type=f32)

    base = step * rows + H
    p_all = p_split[pl.ds(base, rows)]
    p_high_part = p_all[:, :B, :].reshape(rows * B, 2 * GW)
    p_low_part = p_all[:, B:, :].reshape(rows * B, 2 * GW)
    ap_split = [split(ap[g]) for g in range(3)]

    def add(target, lanes):
        for g in range(3):
            high, low = ap_split[g]
            value = product(p_high_part[:, lanes], high)
            value = value + product(p_low_part[:, lanes], high)
            value = value + product(p_high_part[:, lanes], low)
            for half in range(2):
                out_ref[target, 2 * g + half] += value[:, half * LANES : (half + 1) * LANES]

    add(1, slice(0, GW))

    @pl.when(step < H // rows)
    def _():
        add(0, slice(GW, 2 * GW))

    @pl.when(step >= (R - H) // rows)
    def _():
        add(2, slice(GW, 2 * GW))


def coarse_parts(pieces, p_own, p_low, p_high, cols):
    rows = 4
    whole = lambda shape: pl.BlockSpec(shape, lambda i, *_: (0,) * len(shape))
    return pl.pallas_call(
        coarse_kernel,
        out_shape=jax.ShapeDtypeStruct((3, 6, GW, LANES), f32),
        grid_spec=pltpu.PrefetchScalarGridSpec(
            num_scalar_prefetch=1,
            grid=(R // rows,),
            in_specs=[
                pl.BlockSpec((rows, K, B, LANES), lambda i, *_: (i, 0, 0, 0)),
                whole((R, B, 2 * GW)),
                whole((H, B, 2 * GW)),
                whole((H, B, 2 * GW)),
            ],
            out_specs=whole((3, 6, GW, LANES)),
            scratch_shapes=[
                pltpu.VMEM((R + 2 * H, 2 * B, 2 * GW), bf16),
                pltpu.VMEM((3, rows * B, GW), f32),
            ],
        ),
        compiler_params=pltpu.CompilerParams(vmem_limit_bytes=48 << 20),
        name="coarse",
    )(cols, pieces, p_own, p_low, p_high)


def assemble_kernel(pick, own, lower, upper, out_ref):
    for j in range(10):
        terms = []
        if j < 6:
            terms.append(lower[j])
        if 2 <= j < 8:
            terms.append(own[j - 2])
        if j >= 4:
            terms.append(upper[j - 4])
        out_ref[0, j] = functools.reduce(jnp.add, terms)


def assemble(own, lower, upper, pick, slots):
    spec = pl.BlockSpec((6, B, LANES), lambda j, pick: (0, pick[j], 0))
    return pl.pallas_call(
        assemble_kernel,
        out_shape=jax.ShapeDtypeStruct((slots, 10, B, LANES), f32),
        grid_spec=pltpu.PrefetchScalarGridSpec(
            num_scalar_prefetch=1,
            grid=(slots,),
            in_specs=[spec, spec, spec],
            out_specs=pl.BlockSpec((1, 10, B, LANES), lambda j, pick: (j, 0, 0, 0)),
        ),
        name="assemble",
    )(pick, own, lower, upper)


def exchange_kernel(slots, send, codes, recv, got, send_sem, recv_sem, code_send, code_recv, own_sem):
    me = lax.axis_index("col")
    row = lax.axis_index("row")
    barrier = pltpu.get_barrier_semaphore()
    for s in range(1, slots):
        peer = lax.rem(me + s, slots)
        pl.semaphore_signal(
            barrier, inc=1, device_id=(row, peer), device_id_type=pl.DeviceIdType.MESH
        )
    pl.semaphore_wait(barrier, slots - 1)
    copies = []
    for s in range(1, slots):
        peer = lax.rem(me + s, slots)
        for source, target, here, there in (
            (codes, got, code_send, code_recv),
            (send, recv, send_sem, recv_sem),
        ):
            copy = pltpu.make_async_remote_copy(
                src_ref=source.at[peer],
                dst_ref=target.at[me],
                send_sem=here.at[s],
                recv_sem=there.at[s],
                device_id=(row, peer),
                device_id_type=pl.DeviceIdType.MESH,
            )
            copy.start()
            copies.append(copy)
    for index, (source, target) in enumerate(((codes, got), (send, recv))):
        copy = pltpu.make_async_copy(source.at[me], target.at[me], own_sem.at[index])
        copy.start()
        copies.append(copy)
    for copy in copies:
        copy.wait()


def exchange(send, codes, slots):
    anywhere = pl.BlockSpec(memory_space=pl.ANY)
    dma = pltpu.SemaphoreType.DMA
    return pl.pallas_call(
        functools.partial(exchange_kernel, slots),
        out_shape=(
            jax.ShapeDtypeStruct(send.shape, send.dtype),
            jax.ShapeDtypeStruct(codes.shape, codes.dtype),
        ),
        in_specs=[anywhere, anywhere],
        out_specs=(anywhere, anywhere),
        scratch_shapes=[dma((slots,)), dma((slots,)), dma((slots,)), dma((slots,)), dma((2,))],
        compiler_params=pltpu.CompilerParams(collective_id=0, has_side_effects=True),
        name="exchange",
    )(send, codes)


def final_kernel(source, in_ref, out_ref, pairs):
    low = lane_low(B // 2)
    for j in range(5 * G // 2):
        even = in_ref[0, j, pl.ds(0, B // 2, stride=2), :]
        odd = in_ref[0, j, pl.ds(1, B // 2, stride=2), :]
        pairs[pl.ds(2 * j * (B // 2), B // 2), :] = jnp.where(low, even, pltpu.roll(odd, B, 1))
        pairs[pl.ds((2 * j + 1) * (B // 2), B // 2), :] = jnp.where(low, pltpu.roll(even, B, 1), odd)
    for c in range(B // 2):
        out_ref[0, :, c * LANES : (c + 1) * LANES] = pairs[pl.ds(c, 5 * G, stride=B // 2), :]


def final(recv, source):
    return pl.pallas_call(
        final_kernel,
        out_shape=jax.ShapeDtypeStruct((G, 5 * G, BB), f32),
        grid_spec=pltpu.PrefetchScalarGridSpec(
            num_scalar_prefetch=1,
            grid=(G,),
            in_specs=[pl.BlockSpec((1, 10, B, LANES), lambda g, source: (source[g], 0, 0, 0))],
            out_specs=pl.BlockSpec((1, 5 * G, BB), lambda g, source: (g, 0, 0)),
            scratch_shapes=[pltpu.VMEM((5 * G * B // 2, LANES), f32)],
        ),
        name="final",
    )(source, recv)


def shift(value, distance):
    axes = ("row", "col")
    count = lax.axis_size(axes)
    route = [(i, i + distance) for i in range(count) if 0 <= i + distance < count]
    return lax.ppermute(value, axes, route)


def local(a_blocks, columns, tentative, aggregate, owner):
    axes = ("row", "col")
    device = lax.axis_index(axes)
    slots = lax.axis_size("col")
    t_low, t_high = shift(tentative[R - H :], 1), shift(tentative[:H], -1)
    aggs = jnp.concatenate([shift(aggregate[R - H :], 1), aggregate, shift(aggregate[:H], -1)])
    cols = (columns - device * R + H).reshape(-1)
    p_own, pieces = smooth_rows(a_blocks, t_low, tentative, t_high, cols, aggs)
    p_low, p_high = shift(p_own[R - H :], 1), shift(p_own[:H], -1)
    parts = coarse_parts(pieces, p_own, p_low, p_high, cols)
    from_lower, from_upper = shift(parts[2], 1), shift(parts[0], -1)

    target = (owner // G) % slots
    hits = target[None, :] == jnp.arange(slots, dtype=jnp.int32)[:, None]
    pick = jnp.sum(hits * jnp.arange(G, dtype=jnp.int32)[None, :], axis=1).astype(jnp.int32)
    place = jnp.sum(hits * (owner % G + 1)[None, :], axis=1).astype(jnp.int32)
    codes = jnp.broadcast_to(place[:, None, None], (slots, 8, LANES))
    send = assemble(parts[1], from_lower, from_upper, pick, slots)
    recv, got = exchange(send, codes, slots)
    places = got[:, 0, 0]
    wanted = places[None, :] == jnp.arange(1, G + 1, dtype=jnp.int32)[:, None]
    source = jnp.sum(wanted * jnp.arange(slots, dtype=jnp.int32)[None, :], axis=1)
    return final(recv, source.astype(jnp.int32))


def solution(mesh):
    placed = (
        P(("row", "col"), None, None),
        P(("row", "col"), None),
        P(("row", "col"), None),
        P(("row", "col")),
        P(("row", "col")),
    )
    return jax.shard_map(
        local, mesh=mesh, in_specs=placed, out_specs=P(("row", "col"), None, None), check_vma=False
    )
```

```python
import functools

import jax
import jax.numpy as jnp
from jax import lax
from jax.experimental import pallas as pl
from jax.experimental.pallas import tpu as pltpu
from jax.sharding import PartitionSpec as P

B = 64
K = 6
G = 4
R = 32
H = 8
BB = B * B
GW = G * B
LANES = 128
relaxation = 2.0 / 3.0
f32 = jnp.float32
bf16 = jnp.bfloat16


def lane_low(rows):
    return lax.broadcasted_iota(jnp.int32, (rows, LANES), 1) < B


def natural_dup(half_rows, scratch):
    low = lane_low(B // 2)
    swapped = pltpu.roll(half_rows, B, 1)
    scratch[pl.ds(0, B // 2, stride=2), :] = jnp.where(low, half_rows, swapped)
    scratch[pl.ds(1, B // 2, stride=2), :] = jnp.where(low, swapped, half_rows)


def smooth_kernel(cols, aggs, a_ref, t_low, t_own, t_high, p_ref, aa_ref, flat, nat, t_nat, t_split):
    step = pl.program_id(0)
    rows = 8
    low = lane_low(B)

    @pl.when(step == 0)
    def _():
        for chunk in range(R // 8 + 2):
            source = t_low if chunk == 0 else t_high if chunk == R // 8 + 1 else t_own
            first = 0 if chunk in (0, R // 8 + 1) else (chunk - 1) * 8
            for c in range(B // 2):
                flat[pl.ds(c * 8, 8), :] = source[first : first + 8, c * LANES : (c + 1) * LANES]

            def one(j, carry):
                n = chunk * 8 + j
                natural_dup(flat[pl.ds(j, B // 2, stride=8), :], t_nat.at[n])
                value = t_nat[n]
                high = value.astype(bf16)
                t_split[n, 0:B, :] = high
                t_split[n, B : 2 * B, :] = (value - high.astype(f32)).astype(bf16)
                return carry

            lax.fori_loop(0, 8, one, 0)

    sub = lax.broadcasted_iota(jnp.int32, (B, LANES), 0)
    lane = lax.broadcasted_iota(jnp.int32, (B, LANES), 1)
    on_diagonal = sub == lane

    for r in range(rows):
        n = step * rows + r
        for part in range(4):
            p_ref[r, :, part * LANES : (part + 1) * LANES] = jnp.zeros((B, LANES), f32)
        scale = None
        for k in range(K):
            ci = cols[n * K + k]
            tiles = a_ref.at[k, 0].reshape(B // 2 * 8, LANES)
            slot = (r % 2) * K + k
            natural_dup(tiles[pl.ds(r, B // 2, stride=8), :], nat.at[slot])
            value = nat[slot]
            if k == 0:
                diagonal = jnp.sum(jnp.where(on_diagonal, value, 0.0), axis=1, keepdims=True)
                scale = relaxation / diagonal
            high = value.astype(bf16).astype(f32)
            pieces = jnp.where(low, high, value - high).astype(bf16)
            aa_ref[r, k] = pieces
            basis = t_split[ci]
            weights = jnp.concatenate([basis[:B], basis[:B], basis[B:], basis[B:]], axis=0)
            applied = jnp.dot(
                jnp.concatenate([pieces, pieces], axis=1), weights, preferred_element_type=f32
            )
            smooth = -applied * scale
            if k == 0:
                smooth = smooth + t_nat[n + H]
            label = aggs[ci]
            outside = jnp.logical_or(ci < H, ci >= R + H).astype(jnp.int32)
            place = pl.multiple_of((outside * 2 + label // 2) * LANES, LANES)
            keep = jnp.where(low, 1 - label % 2, label % 2) == 1
            window = (r, slice(None), pl.ds(place, LANES))
            p_ref[window] = p_ref[window] + jnp.where(keep, smooth, 0.0)


def smooth_rows(a_blocks, t_low, t_own, t_high, cols, aggs):
    rows = 8
    tiled = a_blocks.reshape(R // rows, rows, K, B // 2, LANES).transpose(2, 0, 3, 1, 4)
    whole = lambda shape: pl.BlockSpec(shape, lambda i, *_: (0,) * len(shape))
    return pl.pallas_call(
        smooth_kernel,
        out_shape=(
            jax.ShapeDtypeStruct((R, B, 2 * GW), f32),
            jax.ShapeDtypeStruct((R, K, B, LANES), bf16),
        ),
        grid_spec=pltpu.PrefetchScalarGridSpec(
            num_scalar_prefetch=2,
            grid=(R // rows,),
            in_specs=[
                pl.BlockSpec((K, 1, B // 2, rows, LANES), lambda i, *_: (0, i, 0, 0, 0)),
                whole((H, BB)),
                whole((R, BB)),
                whole((H, BB)),
            ],
            out_specs=(
                pl.BlockSpec((rows, B, 2 * GW), lambda i, *_: (i, 0, 0)),
                pl.BlockSpec((rows, K, B, LANES), lambda i, *_: (i, 0, 0, 0)),
            ),
            scratch_shapes=[
                pltpu.VMEM((B // 2 * 8, LANES), f32),
                pltpu.VMEM((2 * K, B, LANES), f32),
                pltpu.VMEM((R + 2 * H, B, LANES), f32),
                pltpu.VMEM((R + 2 * H, 2 * B, LANES), bf16),
            ],
        ),
        compiler_params=pltpu.CompilerParams(vmem_limit_bytes=40 << 20),
        name="smooth",
    )(cols, aggs, tiled, t_low, t_own, t_high)


def coarse_kernel(cols, aa_ref, p_own, p_low, p_high, out_ref, p_split, ap):
    step = pl.program_id(0)
    rows = aa_ref.shape[0]

    def split(value):
        high = value.astype(bf16)
        return high, (value - high.astype(f32)).astype(bf16)

    @pl.when(step == 0)
    def _():
        out_ref[...] = jnp.zeros_like(out_ref)

        def own(n, carry):
            high, low = split(p_own[n])
            p_split[n + H, 0:B, :] = high
            p_split[n + H, B : 2 * B, :] = low
            return carry

        lax.fori_loop(0, R, own, 0)
        for source, base in ((p_low, 0), (p_high, R + H)):

            def halo(n, carry, source=source, base=base):
                for half in range(2):
                    high, low = split(source[n, :, (1 - half) * GW : (2 - half) * GW])
                    p_split[base + n, 0:B, half * GW : (half + 1) * GW] = high
                    p_split[base + n, B : 2 * B, half * GW : (half + 1) * GW] = low
                return carry

            lax.fori_loop(0, H, halo, 0)

    ap[0] = jnp.zeros_like(ap[0])
    ap[2] = jnp.zeros_like(ap[2])
    for r in range(rows):
        n = step * rows + r
        total = jnp.zeros((B, GW), f32)
        for k in range(K):
            ci = cols[n * K + k]
            pieces = aa_ref[r, k]
            basis = p_split[ci]
            weights = jnp.concatenate([basis[:B], basis[:B], basis[B:], basis[B:]], axis=0)
            applied = jnp.dot(
                jnp.concatenate([pieces, pieces], axis=1), weights, preferred_element_type=f32
            )
            total = total + applied[:, :GW]
            window = (jnp.where(ci < R // 2, 0, 2), slice(r * B, (r + 1) * B), slice(None))
            ap[window] = ap[window] + applied[:, GW:]
        ap[1, r * B : (r + 1) * B, :] = total

    def product(left, right):
        return lax.dot_general(left, right, (((0,), (0,)), ((), ())), preferred_element_type=f32)

    base = step * rows + H
    p_all = p_split[pl.ds(base, rows)]
    p_high_part = p_all[:, :B, :].reshape(rows * B, 2 * GW)
    p_low_part = p_all[:, B:, :].reshape(rows * B, 2 * GW)
    ap_split = [split(ap[g]) for g in range(3)]

    def add(target, lanes):
        for g in range(3):
            high, low = ap_split[g]
            value = product(p_high_part[:, lanes], high)
            value = value + product(p_low_part[:, lanes], high)
            value = value + product(p_high_part[:, lanes], low)
            for half in range(2):
                tile = value[:, half * LANES : (half + 1) * LANES]
                out_ref[target, :, 2 * g + half] += tile.reshape(G, B, LANES)

    add(1, slice(0, GW))

    @pl.when(step < H // rows)
    def _():
        add(0, slice(GW, 2 * GW))

    @pl.when(step >= (R - H) // rows)
    def _():
        add(2, slice(GW, 2 * GW))


def coarse_parts(pieces, p_own, p_low, p_high, cols):
    rows = 4
    whole = lambda shape: pl.BlockSpec(shape, lambda i, *_: (0,) * len(shape))
    return pl.pallas_call(
        coarse_kernel,
        out_shape=jax.ShapeDtypeStruct((3, G, 6, B, LANES), f32),
        grid_spec=pltpu.PrefetchScalarGridSpec(
            num_scalar_prefetch=1,
            grid=(R // rows,),
            in_specs=[
                pl.BlockSpec((rows, K, B, LANES), lambda i, *_: (i, 0, 0, 0)),
                whole((R, B, 2 * GW)),
                whole((H, B, 2 * GW)),
                whole((H, B, 2 * GW)),
            ],
            out_specs=whole((3, G, 6, B, LANES)),
            scratch_shapes=[
                pltpu.VMEM((R + 2 * H, 2 * B, 2 * GW), bf16),
                pltpu.VMEM((3, rows * B, GW), f32),
            ],
        ),
        compiler_params=pltpu.CompilerParams(vmem_limit_bytes=48 << 20),
        name="coarse",
    )(cols, pieces, p_own, p_low, p_high)


MESH = pl.DeviceIdType.MESH
CHUNKS = 5


def finish_kernel(
    slots, pick, codes, parts, recv, got, lower, upper, send, relay,
    near_send, near_recv, code_send, code_recv, send_sem, recv_sem, hop_send, hop_recv, own_sem,
):
    me, row = lax.axis_index("col"), lax.axis_index("row")
    rows = lax.axis_size("row")
    device, count = row * slots + me, rows * slots

    def place(index):
        return (index // slots, lax.rem(index, slots))

    behind = place(lax.rem(device + count - 1, count))
    ahead = place(lax.rem(device + 1, count))
    peers = [lax.rem(me + s, slots) for s in range(1, slots)]
    barrier = pltpu.get_barrier_semaphore()
    targets = [(row, peer) for peer in peers] + [behind, ahead]
    for target in targets:
        pl.semaphore_signal(barrier, inc=1, device_id=target, device_id_type=MESH)
    pl.semaphore_wait(barrier, len(targets))

    def remote(source, target, here, there, where):
        copy = pltpu.make_async_remote_copy(
            src_ref=source, dst_ref=target, send_sem=here, recv_sem=there,
            device_id=where, device_id_type=MESH,
        )
        copy.start()
        return copy

    near = [
        remote(parts.at[2], lower, near_send.at[0], near_recv.at[0], ahead),
        remote(parts.at[0], upper, near_send.at[1], near_recv.at[1], behind),
    ]
    copies = []
    for s, peer in enumerate(peers):
        copies.append(
            remote(codes.at[peer], got.at[me], code_send.at[s], code_recv.at[s], (row, peer))
        )
    for copy in near:
        copy.wait_recv()

    has_low = (device > 0).astype(f32)
    has_high = (device < count - 1).astype(f32)

    def build(target):
        a = pick[target]
        for j in range(10):
            terms = []
            if j < 6:
                terms.append(lower[a, j] * has_low)
            if 2 <= j < 8:
                terms.append(parts[1, a, j - 2])
            if j >= 4:
                terms.append(upper[a, j - 4] * has_high)
            send[target, j] = functools.reduce(jnp.add, terms)

    core = lax.rem(me, 2)
    chip = me - core
    far = lax.rem(chip + 4, slots)
    before = lax.rem(chip + 6, slots)
    after = lax.rem(chip + 2, slots)
    step = 10 // CHUNKS
    order = [far + core, far + 1 - core, after + core, before + core, after + 1 - core, before + 1 - core, chip + 1 - core]
    for s, peer in enumerate(order):
        build(peer)
        copies.append(
            remote(send.at[peer], recv.at[me], send_sem.at[s], recv_sem.at[s], (row, peer))
        )
    build(me)
    for index, (source, target) in enumerate(((codes, got), (send, recv))):
        copy = pltpu.make_async_copy(source.at[me], target.at[me], own_sem.at[index])
        copy.start()
        copies.append(copy)
    hops, last = [], []
    for copy in near + hops:
        copy.wait_send()
    for copy in copies + last:
        copy.wait()


def finish(parts, pick, codes, slots):
    anywhere = pl.BlockSpec(memory_space=pl.ANY)
    vmem = pl.BlockSpec(memory_space=pltpu.VMEM)
    dma = pltpu.SemaphoreType.DMA
    return pl.pallas_call(
        functools.partial(finish_kernel, slots),
        out_shape=(
            jax.ShapeDtypeStruct((slots, 10, B, LANES), f32),
            jax.ShapeDtypeStruct(codes.shape, codes.dtype),
        ),
        in_specs=[pl.BlockSpec(memory_space=pltpu.SMEM), vmem, vmem],
        out_specs=(anywhere, vmem),
        scratch_shapes=[
            pltpu.VMEM((G, 6, B, LANES), f32),
            pltpu.VMEM((G, 6, B, LANES), f32),
            pltpu.VMEM((slots, 10, B, LANES), f32),
            pltpu.VMEM((10, B, LANES), f32),
            dma((2,)), dma((2,)),
            dma((slots,)), dma((slots,)),
            dma((slots,)), dma((slots,)),
            dma((2 * CHUNKS,)), dma((2 * CHUNKS,)),
            dma((2,)),
        ],
        compiler_params=pltpu.CompilerParams(
            collective_id=0, has_side_effects=True, vmem_limit_bytes=32 << 20
        ),
        name="finish",
    )(pick, codes, parts)


def final_kernel(source, *refs):
    blocks, out_ref, pairs = refs[:G], refs[G], refs[G + 1]
    low = lane_low(B // 2)
    tiles = blocks[0].shape[1]
    for g in range(G):
        for j in range(tiles):
            even = blocks[g][0, j, pl.ds(0, B // 2, stride=2), :]
            odd = blocks[g][0, j, pl.ds(1, B // 2, stride=2), :]
            base = (g * tiles + j) * B
            pairs[pl.ds(base, B // 2), :] = jnp.where(low, even, pltpu.roll(odd, B, 1))
            pairs[pl.ds(base + B // 2, B // 2), :] = jnp.where(low, pltpu.roll(even, B, 1), odd)
    for col in range(2 * tiles):
        for c in range(B // 2):
            rows = pl.ds(col * (B // 2) + c, G, stride=tiles * B)
            out_ref[col, :, c * LANES : (c + 1) * LANES] = pairs[rows, :]


def final(recv, source):
    tiles = 2
    specs = [
        pl.BlockSpec((1, tiles, B, LANES), lambda j, source, g=g: (source[g], j, 0, 0))
        for g in range(G)
    ]
    result = pl.pallas_call(
        final_kernel,
        out_shape=jax.ShapeDtypeStruct((5 * G, G, BB), f32),
        grid_spec=pltpu.PrefetchScalarGridSpec(
            num_scalar_prefetch=1,
            grid=(10 // tiles,),
            in_specs=specs,
            out_specs=pl.BlockSpec((2 * tiles, G, BB), lambda j, source: (j, 0, 0)),
            scratch_shapes=[pltpu.VMEM((G * tiles * B, LANES), f32)],
        ),
        name="final",
    )(source, recv, recv, recv, recv)
    return result.transpose(1, 0, 2)


def shift(value, distance):
    axes = ("row", "col")
    count = lax.axis_size(axes)
    route = [(i, i + distance) for i in range(count) if 0 <= i + distance < count]
    return lax.ppermute(value, axes, route)


def local(a_blocks, columns, tentative, aggregate, owner):
    axes = ("row", "col")
    device = lax.axis_index(axes)
    slots = lax.axis_size("col")
    t_low, t_high = shift(tentative[R - H :], 1), shift(tentative[:H], -1)
    aggs = jnp.concatenate([shift(aggregate[R - H :], 1), aggregate, shift(aggregate[:H], -1)])
    cols = (columns - device * R + H).reshape(-1)
    p_own, pieces = smooth_rows(a_blocks, t_low, tentative, t_high, cols, aggs)
    p_low, p_high = shift(p_own[R - H :], 1), shift(p_own[:H], -1)
    parts = coarse_parts(pieces, p_own, p_low, p_high, cols)
    target = (owner // G) % slots
    hits = target[None, :] == jnp.arange(slots, dtype=jnp.int32)[:, None]
    pick = jnp.sum(hits * jnp.arange(G, dtype=jnp.int32)[None, :], axis=1).astype(jnp.int32)
    place = jnp.sum(hits * (owner % G + 1)[None, :], axis=1).astype(jnp.int32)
    codes = jnp.broadcast_to(place[:, None, None], (slots, 8, LANES))
    recv, got = finish(parts, pick, codes, slots)
    places = got[:, 0, 0]
    wanted = places[None, :] == jnp.arange(1, G + 1, dtype=jnp.int32)[:, None]
    source = jnp.sum(wanted * jnp.arange(slots, dtype=jnp.int32)[None, :], axis=1)
    return final(recv, source.astype(jnp.int32))


def solution(mesh):
    placed = (
        P(("row", "col"), None, None),
        P(("row", "col"), None),
        P(("row", "col"), None),
        P(("row", "col")),
        P(("row", "col")),
    )
    return jax.shard_map(
        local, mesh=mesh, in_specs=placed, out_specs=P(("row", "col"), None, None), check_vma=False
    )
```

```python
import functools

import jax
import jax.numpy as jnp
from jax import lax
from jax.experimental import pallas as pl
from jax.experimental.pallas import tpu as pltpu
from jax.sharding import PartitionSpec as P

B = 64
K = 6
G = 4
R = 32
H = 8
BB = B * B
GW = G * B
LANES = 128
WIDE = K // 2 * 3 * LANES
relaxation = 2.0 / 3.0
f32 = jnp.float32
bf16 = jnp.bfloat16


def lane_low(rows):
    return lax.broadcasted_iota(jnp.int32, (rows, LANES), 1) < B


def natural_dup(half_rows, scratch):
    low = lane_low(B // 2)
    swapped = pltpu.roll(half_rows, B, 1)
    scratch[pl.ds(0, B // 2, stride=2), :] = jnp.where(low, half_rows, swapped)
    scratch[pl.ds(1, B // 2, stride=2), :] = jnp.where(low, swapped, half_rows)


MESH = pl.DeviceIdType.MESH
PIECES = 5
ROWS = 4
CHUNK = ROWS * B


def split(value):
    high = value.astype(bf16)
    return high, (value - high.astype(f32)).astype(bf16)


def coarse_kernel(
    slots, columns, aggregate, owner, a_hbm, t_hbm, recv, got,
    a_tiles, t_tiles, t_nat, t_split, labels, codes, nat, smooth, aa, p_own,
    p_low, p_high, p_split, ap, own, below_out, above_out,
    lower_0, lower_1, lower_2, upper_0, upper_1, upper_2, label_rims, send,
    load_sem, rim_send, rim_recv, halo_send, halo_recv, near_send, near_recv, code_send, code_recv, row_send, row_recv, own_sem,
):
    me, row = lax.axis_index("col"), lax.axis_index("row")
    rows = lax.axis_size("row")
    device, count = row * slots + me, rows * slots

    def place(index):
        return (index // slots, lax.rem(index, slots))

    behind = place(lax.rem(device + count - 1, count))
    ahead = place(lax.rem(device + 1, count))
    lower, upper = (lower_0, lower_1, lower_2), (upper_0, upper_1, upper_2)
    core = lax.rem(me, 2)
    chip = me - core
    far, before, after = (lax.rem(chip + d, slots) for d in (4, 6, 2))
    peers = [far + core, far + 1 - core, after + core, before + core]
    peers += [after + 1 - core, before + 1 - core, chip + 1 - core]

    def load(source, target, index):
        copy = pltpu.make_async_copy(source, target, load_sem.at[index])
        copy.start()
        return copy

    half = pl.ds(0, B // 2)
    t_load = load(t_hbm, t_tiles.at[pl.ds(1, R // 8), half], 0)
    order = (1, 2, 0, 3)
    a_load = {tile: load(a_hbm.at[:, tile], a_tiles.at[tile, :, half], 1 + tile) for tile in order}
    for n in range(R):
        labels[n + H] = jnp.full((8, LANES), aggregate[n], jnp.int32)

    def here(target, i):
        return (lax.rem(lax.div(owner[i], G), slots) == target).astype(jnp.int32)

    for target in range(slots):
        code = sum(here(target, i) * (lax.rem(owner[i], G) + 1) for i in range(G))
        codes[target] = jnp.full((8, LANES), code, jnp.int32)
    barrier = pltpu.get_barrier_semaphore()
    targets = [(row, peer) for peer in peers] + [behind, ahead]
    for target in targets:
        pl.semaphore_signal(barrier, inc=1, device_id=target, device_id_type=MESH)
    pl.semaphore_wait(barrier, len(targets))

    def remote(source, target, here, there, where):
        copy = pltpu.make_async_remote_copy(
            src_ref=source, dst_ref=target, send_sem=here, recv_sem=there,
            device_id=where, device_id_type=MESH,
        )
        copy.start()
        return copy

    rims = [
        remote(t_hbm.at[R // 8 - 1], t_tiles.at[0, half], rim_send.at[0], rim_recv.at[0], ahead),
        remote(t_hbm.at[0], t_tiles.at[R // 8 + 1, half], rim_send.at[1], rim_recv.at[1], behind),
        remote(
            labels.at[pl.ds(R, H)], label_rims.at[0], rim_send.at[2], rim_recv.at[2], ahead
        ),
        remote(
            labels.at[pl.ds(H, H)], label_rims.at[1], rim_send.at[3], rim_recv.at[3],
            behind,
        ),
    ]
    copies = []
    for s, peer in enumerate(peers):
        copies.append(
            remote(codes.at[peer], got.at[me], code_send.at[s], code_recv.at[s], (row, peer))
        )
    has_low = (device > 0).astype(f32)
    has_high = (device < count - 1).astype(f32)

    low = lane_low(B)
    sub = lax.broadcasted_iota(jnp.int32, (B, LANES), 0)
    lane = lax.broadcasted_iota(jnp.int32, (B, LANES), 1)
    on_diagonal = sub == lane
    second = (lax.broadcasted_iota(jnp.int32, (8, LANES), 1) >= B).astype(jnp.int32)

    def split_basis(chunk):
        tiles = t_tiles.at[chunk].reshape((B // 2 + 1) * 8, LANES)

        def one(j, carry):
            n = chunk * 8 + j
            natural_dup(tiles[pl.ds(j, B // 2, stride=8), :], t_nat.at[n])
            high, rest = split(t_nat[n, 0:B, :])
            t_split[n, 0:B, :] = high
            t_split[n, B : 2 * B, :] = rest
            return carry

        lax.fori_loop(0, 8, one, 0)

    def column(n, k):
        return jnp.clip(columns[k, n] - device * R + H, 0, R + 2 * H - 1)

    def smooth_rows(tile):
        def one(r, carry):
            n = tile * 8 + r
            scale, previous, masks = None, None, []
            for k in range(K):
                ci = column(n, k)
                tiles = a_tiles.at[tile, k].reshape((B // 2 + 1) * 8, LANES)
                natural_dup(tiles[pl.ds(r, B // 2, stride=8), :], nat.at[k])
                value = nat[k, 0:B, :]
                if k == 0:
                    diagonal = jnp.sum(jnp.where(on_diagonal, value, 0.0), axis=1, keepdims=True)
                    scale = relaxation / diagonal
                high = value.astype(bf16).astype(f32)
                pieces = jnp.where(low, high, value - high).astype(bf16)
                base = (k // 2) * 3 * LANES
                aa[n, :, base + (k % 2) * LANES : base + (k % 2 + 1) * LANES] = pieces
                if k % 2 == 1:
                    both = jnp.where(low, previous, high).astype(bf16)
                    aa[n, :, base + 2 * LANES : base + 3 * LANES] = both
                previous = high
                basis = t_split[ci]
                weights = jnp.concatenate([basis[:B], basis[:B], basis[B:], basis[B:]], axis=0)
                applied = jnp.dot(
                    jnp.concatenate([pieces, pieces], axis=1), weights, preferred_element_type=f32
                )
                result = -applied * scale
                if k == 0:
                    result = result + t_nat[n + H, 0:B, :]
                smooth[k] = result.reshape(B // 8, 8, LANES)
                outside = jnp.logical_or(ci < H, ci >= R + H).astype(jnp.int32)
                masks.append(labels[ci] + outside * G)
            for part in range(4):
                total = None
                for k in range(K):
                    keep = masks[k] == 2 * part + second
                    term = jnp.where(keep[None], smooth[k], 0.0)
                    total = term if total is None else total + term
                p_own[n, :, part * LANES : (part + 1) * LANES] = total.reshape(B, LANES)
            return carry

        lax.fori_loop(0, 8, one, 0)

    t_load.wait()
    for chunk in range(1, R // 8 + 1):
        split_basis(chunk)
    for tile in (1, 2):
        a_load[tile].wait()
        smooth_rows(tile)
    for copy in rims:
        copy.wait_recv()
    labels[0:H] = label_rims[0]
    labels[R + H : R + 2 * H] = label_rims[1]
    split_basis(0)
    split_basis(R // 8 + 1)
    for tile in (0, 3):
        a_load[tile].wait()
        smooth_rows(tile)
    halo = [
        remote(p_own.at[pl.ds(R - H, H)], p_low, halo_send.at[0], halo_recv.at[0], ahead),
        remote(p_own.at[pl.ds(0, H)], p_high, halo_send.at[1], halo_recv.at[1], behind),
    ]

    def split_own(n, carry):
        high, low = split(p_own[n])
        p_split[n + H, 0:B, :] = high
        p_split[n + H, B : 2 * B, :] = low
        return carry

    lax.fori_loop(0, R, split_own, 0)
    own[...] = jnp.zeros_like(own)

    def applied_rows(chunk, slot):
        for r in range(ROWS):
            n = chunk * ROWS + r
            weights, marks = [], []
            for pair in range(K // 2):
                index = [column(n, 2 * pair + t) for t in range(2)]
                basis = [p_split[ci] for ci in index]
                side = [(ci < R // 2).astype(f32) for ci in index]
                for t in range(2):
                    marks.append(jnp.full((B, LANES), side[t], f32))
                    weights.extend([basis[t][:B], basis[t][:B]])
                marks.append(jnp.where(lane_low(B), side[0], side[1]))
                weights.extend([basis[0][B:], basis[1][B:]])
            left = aa[n]
            marks = jnp.concatenate(marks, axis=1).astype(bf16)
            weights = jnp.concatenate(weights, axis=0)
            below = left * marks
            middle = jnp.dot(left, weights[:, :GW], preferred_element_type=f32)
            sides = jnp.dot(
                jnp.concatenate([below, left - below], axis=0),
                weights[:, GW:],
                preferred_element_type=f32,
            )
            for g, value in enumerate((sides[:B], middle, sides[B:])):
                high, low = split(value)
                ap[slot, 0, r * B : (r + 1) * B, g * GW : (g + 1) * GW] = high
                ap[slot, 1, r * B : (r + 1) * B, g * GW : (g + 1) * GW] = low

    def turned(chunk, part):
        block = p_own[pl.ds(chunk * ROWS, ROWS), :, part * GW : (part + 1) * GW]
        return split(block.reshape(CHUNK, GW).T)

    def product(left, slot, lanes):
        high, low = left
        value = jnp.dot(high, ap[slot, 0, :, lanes], preferred_element_type=f32)
        value = value + jnp.dot(low, ap[slot, 0, :, lanes], preferred_element_type=f32)
        return value + jnp.dot(high, ap[slot, 1, :, lanes], preferred_element_type=f32)

    def add_own(chunk, slot):
        value = product(turned(chunk, 0), slot, slice(0, 3 * GW))
        for t in range(6):
            tile = value[:, t * LANES : (t + 1) * LANES].reshape(G, B, LANES)
            own[t // 2, :, t % 2] += tile

    def inner(chunk, carry):
        applied_rows(chunk, 0)
        add_own(chunk, 0)
        return carry

    lax.fori_loop(H // ROWS, (R - H) // ROWS, inner, 0)

    for copy in halo:
        copy.wait_recv()
    for source, base in ((p_low, 0), (p_high, R + H)):

        def split_halo(n, carry, source=source, base=base):
            for half in range(2):
                high, low = split(source[n, :, (1 - half) * GW : (2 - half) * GW])
                p_split[base + n, 0:B, half * GW : (half + 1) * GW] = high
                p_split[base + n, B : 2 * B, half * GW : (half + 1) * GW] = low
            return carry

        lax.fori_loop(0, H, split_halo, 0)

    def rim_chunk(index):
        return index + (index // 2) * 4

    def rim(index, carry):
        applied_rows(rim_chunk(index), index)
        return carry

    lax.fori_loop(0, 4, rim, 0)

    left_below = [turned(rim_chunk(index), 1) for index in (0, 1)]
    left_above = [turned(rim_chunk(index), 1) for index in (2, 3)]
    near = {}
    for turn in range(3):
        for side, lefts, out, landing, g, base, where in (
            (0, left_above, above_out, lower, turn, 2, ahead),
            (1, left_below, below_out, upper, 2 - turn, 0, behind),
        ):
            lanes = slice(g * GW, (g + 1) * GW)
            value = product(lefts[0], base, lanes) + product(lefts[1], base + 1, lanes)
            for half in range(2):
                tile = value[:, half * LANES : (half + 1) * LANES].reshape(G, B, LANES)
                out[g, :, half] = tile
            near[side, g] = remote(
                out.at[g], landing[g], near_send.at[side, g], near_recv.at[side, g], where
            )
    for index in range(4):
        add_own(rim_chunk(index), index)

    def build(target, piece):
        a = functools.reduce(jnp.maximum, [here(target, i) * i for i in range(1, G)])
        for half in range(2):
            terms = []
            if piece < 3:
                terms.append(lower[piece][a, half] * has_low)
            if 1 <= piece < 4:
                terms.append(own[piece - 1, a, half])
            if piece >= 2:
                terms.append(upper[piece - 2][a, half] * has_high)
            send[target, piece, half] = functools.reduce(jnp.add, terms)

    needs = {0: [(0, 0)], 4: [(1, 2)], 1: [(0, 1)], 3: [(1, 1)], 2: [(0, 2), (1, 0)]}
    for piece in (0, 4, 1, 3, 2):
        for key in needs[piece]:
            near[key].wait_recv()
        for s, peer in enumerate(peers):
            build(peer, piece)
            copies.append(
                remote(
                    send.at[peer, piece], recv.at[me, piece],
                    row_send.at[piece, s], row_recv.at[piece, s], (row, peer),
                )
            )
        build(me, piece)
    for index, (source, target) in enumerate(((codes, got), (send, recv))):
        copy = pltpu.make_async_copy(source.at[me], target.at[me], own_sem.at[index])
        copy.start()
        copies.append(copy)
    for copy in rims + halo + list(near.values()):
        copy.wait_send()
    for copy in copies:
        copy.wait()


def coarse_rows(columns, aggregate, owner, a_blocks, tentative, slots):
    anywhere = pl.BlockSpec(memory_space=pl.ANY)
    vmem = pl.BlockSpec(memory_space=pltpu.VMEM)
    smem = pl.BlockSpec(memory_space=pltpu.SMEM)
    dma = pltpu.SemaphoreType.DMA
    part = pltpu.VMEM((3, G, 2, B, LANES), f32)
    piece = pltpu.VMEM((G, 2, B, LANES), f32)
    a_tiled = a_blocks.reshape(R // 8, 8, K, B // 2, LANES).transpose(2, 0, 3, 1, 4)
    t_tiled = tentative.reshape(R // 8, 8, B // 2, LANES).transpose(0, 2, 1, 3)
    return pl.pallas_call(
        functools.partial(coarse_kernel, slots),
        out_shape=(
            jax.ShapeDtypeStruct((slots, PIECES, 2, B, LANES), f32),
            jax.ShapeDtypeStruct((slots, 8, LANES), jnp.int32),
        ),
        in_specs=[smem, smem, smem, anywhere, anywhere],
        out_specs=(anywhere, vmem),
        scratch_shapes=[
            pltpu.VMEM((R // 8, K, B // 2 + 1, 8, LANES), f32),
            pltpu.VMEM((R // 8 + 2, B // 2 + 1, 8, LANES), f32),
            pltpu.VMEM((R + 2 * H, B + 8, LANES), f32),
            pltpu.VMEM((R + 2 * H, 2 * B, LANES), bf16),
            pltpu.VMEM((R + 2 * H, 8, LANES), jnp.int32),
            pltpu.VMEM((slots, 8, LANES), jnp.int32),
            pltpu.VMEM((K, B + 8, LANES), f32),
            pltpu.VMEM((K, B // 8, 8, LANES), f32),
            pltpu.VMEM((R, B, WIDE), bf16),
            pltpu.VMEM((R, B, 2 * GW), f32),
            pltpu.VMEM((H, B, 2 * GW), f32),
            pltpu.VMEM((H, B, 2 * GW), f32),
            pltpu.VMEM((R + 2 * H, 2 * B, 2 * GW), bf16),
            pltpu.VMEM((4, 2, CHUNK, 3 * GW), bf16),
            part, part, part,
            piece, piece, piece, piece, piece, piece,
            pltpu.VMEM((2, H, 8, LANES), jnp.int32),
            pltpu.VMEM((slots, PIECES, 2, B, LANES), f32),
            dma((1 + R // 8,)),
            dma((4,)), dma((4,)),
            dma((2,)), dma((2,)),
            dma((2, 3)), dma((2, 3)),
            dma((slots,)), dma((slots,)),
            dma((PIECES, slots)), dma((PIECES, slots)),
            dma((2,)),
        ],
        compiler_params=pltpu.CompilerParams(
            collective_id=0, has_side_effects=True, vmem_limit_bytes=48 << 20
        ),
        name="coarse",
    )(columns.T, aggregate, owner, a_tiled, t_tiled)


def final_kernel(source, *refs):
    blocks, out_ref, pairs = refs[:G], refs[G], refs[G + 1]
    low = lane_low(B // 2)
    tiles = 2
    for g in range(G):
        for j in range(tiles):
            even = blocks[g][0, 0, j, pl.ds(0, B // 2, stride=2), :]
            odd = blocks[g][0, 0, j, pl.ds(1, B // 2, stride=2), :]
            base = (g * tiles + j) * B
            pairs[pl.ds(base, B // 2), :] = jnp.where(low, even, pltpu.roll(odd, B, 1))
            pairs[pl.ds(base + B // 2, B // 2), :] = jnp.where(low, pltpu.roll(even, B, 1), odd)
    for col in range(2 * tiles):
        for c in range(B // 2):
            rows = pl.ds(col * (B // 2) + c, G, stride=tiles * B)
            out_ref[col, :, c * LANES : (c + 1) * LANES] = pairs[rows, :]


def final(recv, source):
    tiles = 2
    specs = [
        pl.BlockSpec((1, 1, tiles, B, LANES), lambda j, source, g=g: (source[g], j, 0, 0, 0))
        for g in range(G)
    ]
    result = pl.pallas_call(
        final_kernel,
        out_shape=jax.ShapeDtypeStruct((5 * G, G, BB), f32),
        grid_spec=pltpu.PrefetchScalarGridSpec(
            num_scalar_prefetch=1,
            grid=(PIECES,),
            in_specs=specs,
            out_specs=pl.BlockSpec((2 * tiles, G, BB), lambda j, source: (j, 0, 0)),
            scratch_shapes=[pltpu.VMEM((2 * G * tiles * B, LANES), f32)],
        ),
        name="final",
    )(source, recv, recv, recv, recv)
    return result.transpose(1, 0, 2)


def local(a_blocks, columns, tentative, aggregate, owner):
    slots = lax.axis_size("col")
    recv, got = coarse_rows(columns, aggregate, owner, a_blocks, tentative, slots)
    places = got[:, 0, 0]
    wanted = places[None, :] == jnp.arange(1, G + 1, dtype=jnp.int32)[:, None]
    source = jnp.sum(wanted * jnp.arange(slots, dtype=jnp.int32)[None, :], axis=1)
    return final(recv, source.astype(jnp.int32))


def solution(mesh):
    placed = (
        P(("row", "col"), None, None),
        P(("row", "col"), None),
        P(("row", "col"), None),
        P(("row", "col")),
        P(("row", "col")),
    )
    return jax.shard_map(
        local, mesh=mesh, in_specs=placed, out_specs=P(("row", "col"), None, None), check_vma=False
    )
```

```python
import functools

import jax
import jax.numpy as jnp
from jax import lax
from jax.experimental import pallas as pl
from jax.experimental.pallas import tpu as pltpu
from jax.sharding import PartitionSpec as P

B = 64
K = 6
G = 4
R = 32
H = 8
BB = B * B
GW = G * B
LANES = 128
WIDE = K // 2 * 3 * LANES
relaxation = 2.0 / 3.0
f32 = jnp.float32
bf16 = jnp.bfloat16


def lane_low(rows):
    return lax.broadcasted_iota(jnp.int32, (rows, LANES), 1) < B


def natural_dup(half_rows, scratch):
    low = lane_low(B // 2)
    swapped = pltpu.roll(half_rows, B, 1)
    scratch[pl.ds(0, B // 2, stride=2), :] = jnp.where(low, half_rows, swapped)
    scratch[pl.ds(1, B // 2, stride=2), :] = jnp.where(low, swapped, half_rows)


MESH = pl.DeviceIdType.MESH
PIECES = 5
ROWS = 4
CHUNK = ROWS * B


def split(value):
    high = value.astype(bf16)
    return high, (value - high.astype(f32)).astype(bf16)


def coarse_kernel(
    slots, columns, aggregate, owner, a_hbm, t_hbm, out_ref,
    a_tiles, t_tiles, t_nat, t_split, labels, codes, nat, smooth, aa, p_own,
    p_low, p_high, p_split, ap, own, below_out, above_out,
    lower_0, lower_1, lower_2, upper_0, upper_1, upper_2, label_rims, send, recv, got, chosen, pairs,
    load_sem, rim_send, rim_recv, halo_send, halo_recv, near_send, near_recv, code_send, code_recv, row_send, row_recv,
):
    me, row = lax.axis_index("col"), lax.axis_index("row")
    rows = lax.axis_size("row")
    device, count = row * slots + me, rows * slots

    def place(index):
        return (index // slots, lax.rem(index, slots))

    behind = place(lax.rem(device + count - 1, count))
    ahead = place(lax.rem(device + 1, count))
    lower, upper = (lower_0, lower_1, lower_2), (upper_0, upper_1, upper_2)
    core = lax.rem(me, 2)
    chip = me - core
    far, before, after = (lax.rem(chip + d, slots) for d in (4, 6, 2))
    peers = [far + core, far + 1 - core, after + core, before + core]
    peers += [after + 1 - core, before + 1 - core, chip + 1 - core]

    def load(source, target, index):
        copy = pltpu.make_async_copy(source, target, load_sem.at[index])
        copy.start()
        return copy

    half = pl.ds(0, B // 2)
    t_load = load(t_hbm, t_tiles.at[pl.ds(1, R // 8), half], 0)
    order = (1, 0, 3, 2)
    a_load = {tile: load(a_hbm.at[:, tile], a_tiles.at[tile, :, half], 1 + tile) for tile in order}
    for n in range(R):
        labels[n + H] = jnp.full((8, LANES), aggregate[n], jnp.int32)

    def here(target, i):
        return (lax.rem(lax.div(owner[i], G), slots) == target).astype(jnp.int32)

    for target in range(slots):
        code = sum(here(target, i) * (lax.rem(owner[i], G) + 1) for i in range(G))
        codes[target] = jnp.full((8, LANES), code, jnp.int32)
    barrier = pltpu.get_barrier_semaphore()
    targets = [(row, peer) for peer in peers] + [behind, ahead]
    for target in targets:
        pl.semaphore_signal(barrier, inc=1, device_id=target, device_id_type=MESH)
    pl.semaphore_wait(barrier, len(targets))

    def remote(source, target, here, there, where):
        copy = pltpu.make_async_remote_copy(
            src_ref=source, dst_ref=target, send_sem=here, recv_sem=there,
            device_id=where, device_id_type=MESH,
        )
        copy.start()
        return copy

    rims = [
        remote(t_hbm.at[R // 8 - 1], t_tiles.at[0, half], rim_send.at[0], rim_recv.at[0], ahead),
        remote(t_hbm.at[0], t_tiles.at[R // 8 + 1, half], rim_send.at[1], rim_recv.at[1], behind),
        remote(
            labels.at[pl.ds(R, H)], label_rims.at[0], rim_send.at[2], rim_recv.at[2], ahead
        ),
        remote(
            labels.at[pl.ds(H, H)], label_rims.at[1], rim_send.at[3], rim_recv.at[3],
            behind,
        ),
    ]
    copies = []
    for s, peer in enumerate(peers):
        copies.append(
            remote(codes.at[peer], got.at[me], code_send.at[s], code_recv.at[s], (row, peer))
        )
    has_low = (device > 0).astype(f32)
    has_high = (device < count - 1).astype(f32)

    low = lane_low(B)
    sub = lax.broadcasted_iota(jnp.int32, (B, LANES), 0)
    lane = lax.broadcasted_iota(jnp.int32, (B, LANES), 1)
    on_diagonal = sub == lane
    second = (lax.broadcasted_iota(jnp.int32, (8, LANES), 1) >= B).astype(jnp.int32)

    def split_basis(chunk):
        tiles = t_tiles.at[chunk].reshape((B // 2 + 1) * 8, LANES)

        def one(j, carry):
            n = chunk * 8 + j
            natural_dup(tiles[pl.ds(j, B // 2, stride=8), :], t_nat.at[n])
            high, rest = split(t_nat[n, 0:B, :])
            t_split[n, 0:B, :] = high
            t_split[n, B : 2 * B, :] = rest
            return carry

        lax.fori_loop(0, 8, one, 0)

    def column(n, k):
        return jnp.clip(columns[k, n] - device * R + H, 0, R + 2 * H - 1)

    def smooth_rows(tile):
        def one(r, carry):
            n = tile * 8 + r
            scale, previous, masks = None, None, []
            for k in range(K):
                ci = column(n, k)
                tiles = a_tiles.at[tile, k].reshape((B // 2 + 1) * 8, LANES)
                natural_dup(tiles[pl.ds(r, B // 2, stride=8), :], nat.at[k])
                value = nat[k, 0:B, :]
                if k == 0:
                    diagonal = jnp.sum(jnp.where(on_diagonal, value, 0.0), axis=1, keepdims=True)
                    scale = relaxation / diagonal
                high = value.astype(bf16).astype(f32)
                pieces = jnp.where(low, high, value - high).astype(bf16)
                base = (k // 2) * 3 * LANES
                aa[n, :, base + (k % 2) * LANES : base + (k % 2 + 1) * LANES] = pieces
                if k % 2 == 1:
                    both = jnp.where(low, previous, high).astype(bf16)
                    aa[n, :, base + 2 * LANES : base + 3 * LANES] = both
                previous = high
                basis = t_split[ci]
                weights = jnp.concatenate([basis[:B], basis[:B], basis[B:], basis[B:]], axis=0)
                applied = jnp.dot(
                    jnp.concatenate([pieces, pieces], axis=1), weights, preferred_element_type=f32
                )
                result = -applied * scale
                if k == 0:
                    result = result + t_nat[n + H, 0:B, :]
                smooth[k] = result.reshape(B // 8, 8, LANES)
                outside = jnp.logical_or(ci < H, ci >= R + H).astype(jnp.int32)
                masks.append(labels[ci] + outside * G)
            for part in range(4):
                total = None
                for k in range(K):
                    keep = masks[k] == 2 * part + second
                    term = jnp.where(keep[None], smooth[k], 0.0)
                    total = term if total is None else total + term
                p_own[n, :, part * LANES : (part + 1) * LANES] = total.reshape(B, LANES)
            return carry

        lax.fori_loop(0, 8, one, 0)

    t_load.wait()
    for chunk in range(1, R // 8 + 1):
        split_basis(chunk)
    def smooth_tile(tile):
        a_load[tile].wait()
        smooth_rows(tile)

    smooth_tile(1)
    for copy in rims:
        copy.wait_recv()
    labels[0:H] = label_rims[0]
    labels[R + H : R + 2 * H] = label_rims[1]
    split_basis(0)
    smooth_tile(0)
    halo_low = remote(p_own.at[pl.ds(0, H)], p_high, halo_send.at[1], halo_recv.at[1], behind)
    split_basis(R // 8 + 1)
    smooth_tile(3)
    halo_high = remote(
        p_own.at[pl.ds(R - H, H)], p_low, halo_send.at[0], halo_recv.at[0], ahead
    )
    smooth_tile(2)
    halo = [halo_low, halo_high]

    def split_own(n, carry):
        high, low = split(p_own[n])
        p_split[n + H, 0:B, :] = high
        p_split[n + H, B : 2 * B, :] = low
        return carry

    lax.fori_loop(0, R, split_own, 0)
    own[...] = jnp.zeros_like(own)

    def applied_rows(chunk, slot):
        for r in range(ROWS):
            n = chunk * ROWS + r
            weights, marks = [], []
            for pair in range(K // 2):
                index = [column(n, 2 * pair + t) for t in range(2)]
                basis = [p_split[ci] for ci in index]
                side = [(ci < R // 2).astype(f32) for ci in index]
                for t in range(2):
                    marks.append(jnp.full((B, LANES), side[t], f32))
                    weights.extend([basis[t][:B], basis[t][:B]])
                marks.append(jnp.where(lane_low(B), side[0], side[1]))
                weights.extend([basis[0][B:], basis[1][B:]])
            left = aa[n]
            marks = jnp.concatenate(marks, axis=1).astype(bf16)
            weights = jnp.concatenate(weights, axis=0)
            below = left * marks
            middle = jnp.dot(left, weights[:, :GW], preferred_element_type=f32)
            sides = jnp.dot(
                jnp.concatenate([below, left - below], axis=0),
                weights[:, GW:],
                preferred_element_type=f32,
            )
            for g, value in enumerate((sides[:B], middle, sides[B:])):
                high, low = split(value)
                ap[slot, 0, r * B : (r + 1) * B, g * GW : (g + 1) * GW] = high
                ap[slot, 1, r * B : (r + 1) * B, g * GW : (g + 1) * GW] = low

    def turned(chunk, part):
        block = p_own[pl.ds(chunk * ROWS, ROWS), :, part * GW : (part + 1) * GW]
        return split(block.reshape(CHUNK, GW).T)

    def product(left, slot, lanes):
        high, low = left
        value = jnp.dot(high, ap[slot, 0, :, lanes], preferred_element_type=f32)
        value = value + jnp.dot(low, ap[slot, 0, :, lanes], preferred_element_type=f32)
        return value + jnp.dot(high, ap[slot, 1, :, lanes], preferred_element_type=f32)

    def add_own(chunk, slot):
        value = product(turned(chunk, 0), slot, slice(0, 3 * GW))
        for t in range(6):
            tile = value[:, t * LANES : (t + 1) * LANES].reshape(G, B, LANES)
            own[t // 2, :, t % 2] += tile

    def inner(chunk, carry):
        applied_rows(chunk, 0)
        add_own(chunk, 0)
        return carry

    lax.fori_loop(H // ROWS, (R - H) // ROWS, inner, 0)

    for copy in halo:
        copy.wait_recv()
    for source, base in ((p_low, 0), (p_high, R + H)):

        def split_halo(n, carry, source=source, base=base):
            for half in range(2):
                high, low = split(source[n, :, (1 - half) * GW : (2 - half) * GW])
                p_split[base + n, 0:B, half * GW : (half + 1) * GW] = high
                p_split[base + n, B : 2 * B, half * GW : (half + 1) * GW] = low
            return carry

        lax.fori_loop(0, H, split_halo, 0)

    near = {}

    def rim(first, side, out, landing, turns, where):
        def one(index, carry):
            applied_rows(first + index, 2 * side + index)
            return carry

        lax.fori_loop(0, 2, one, 0)
        lefts = [turned(first + index, 1) for index in range(2)]
        for g in turns:
            lanes = slice(g * GW, (g + 1) * GW)
            value = product(lefts[0], 2 * side, lanes) + product(lefts[1], 2 * side + 1, lanes)
            for half in range(2):
                tile = value[:, half * LANES : (half + 1) * LANES].reshape(G, B, LANES)
                out[g, :, half] = tile
            near[side, g] = remote(
                out.at[g], landing[g], near_send.at[side, g], near_recv.at[side, g], where
            )

    rim((R - H) // ROWS, 0, above_out, lower, (0, 1, 2), ahead)
    rim(0, 1, below_out, upper, (2, 1, 0), behind)

    def sum_own():
        for index in range(2):
            add_own((R - H) // ROWS + index, index)
            add_own(index, 2 + index)

    def build(target, piece):
        a = functools.reduce(jnp.maximum, [here(target, i) * i for i in range(1, G)])
        for half in range(2):
            terms = []
            if piece < 3:
                terms.append(lower[piece][a, half] * has_low)
            if 1 <= piece < 4:
                terms.append(own[piece - 1, a, half])
            if piece >= 2:
                terms.append(upper[piece - 2][a, half] * has_high)
            send[target, piece, half] = functools.reduce(jnp.add, terms)

    needs = {0: [(0, 0)], 4: [(1, 2)], 1: [(0, 1)], 3: [(1, 1)], 2: [(0, 2), (1, 0)]}
    pieces_order = (0, 4, 1, 3, 2)
    arrivals = {}
    for step, piece in enumerate(pieces_order):
        if step == 1:
            sum_own()
        for key in needs[piece]:
            near[key].wait_recv()
        arrivals[piece] = []
        for s, peer in enumerate(peers):
            build(peer, piece)
            arrivals[piece].append(
                remote(
                    send.at[peer, piece], recv.at[me, piece],
                    row_send.at[piece, s], row_recv.at[piece, s], (row, peer),
                )
            )
        build(me, piece)

    for copy in copies:
        copy.wait_recv()
    half_low = lane_low(B // 2)
    for piece in pieces_order:
        for copy in arrivals[piece]:
            copy.wait_recv()
        for half in range(2):
            totals = [None] * G
            for index in range(slots):
                if index == slots - 1:
                    code, block = codes[me], send[me, piece, half]
                else:
                    code, block = got[peers[index]], recv[peers[index], piece, half]
                block = block.reshape(B // 8, 8, LANES)
                for g in range(G):
                    term = jnp.where((code == g + 1)[None], block, 0.0)
                    totals[g] = term if totals[g] is None else totals[g] + term
            for g in range(G):
                chosen[g, half, 0:B, :] = totals[g].reshape(B, LANES)
        for g in range(G):
            for half in range(2):
                even = chosen[g, half, pl.ds(0, B // 2, stride=2), :]
                odd = chosen[g, half, pl.ds(1, B // 2, stride=2), :]
                base = (g * 2 + half) * B
                pairs[base : base + B // 2, :] = jnp.where(
                    half_low, even, pltpu.roll(odd, B, 1)
                )
                pairs[base + B // 2 : base + B, :] = jnp.where(
                    half_low, pltpu.roll(even, B, 1), odd
                )

        def write(c, carry, piece=piece):
            lanes = pl.ds(pl.multiple_of(c * LANES, LANES), LANES)
            for col in range(4):
                rows_of = pl.ds(col * (B // 2) + c, G, stride=2 * B)
                out_ref[piece * 4 + col, :, lanes] = pairs[rows_of, :]
            return carry

        lax.fori_loop(0, B // 2, write, 0, unroll=4)
    for copy in rims + halo + list(near.values()) + copies:
        copy.wait_send()
    for piece in pieces_order:
        for copy in arrivals[piece]:
            copy.wait_send()


def coarse_rows(columns, aggregate, owner, a_blocks, tentative, slots):
    anywhere = pl.BlockSpec(memory_space=pl.ANY)
    vmem = pl.BlockSpec(memory_space=pltpu.VMEM)
    smem = pl.BlockSpec(memory_space=pltpu.SMEM)
    dma = pltpu.SemaphoreType.DMA
    part = pltpu.VMEM((3, G, 2, B, LANES), f32)
    piece = pltpu.VMEM((G, 2, B, LANES), f32)
    a_tiled = a_blocks.reshape(R // 8, 8, K, B // 2, LANES).transpose(2, 0, 3, 1, 4)
    t_tiled = tentative.reshape(R // 8, 8, B // 2, LANES).transpose(0, 2, 1, 3)
    return pl.pallas_call(
        functools.partial(coarse_kernel, slots),
        out_shape=jax.ShapeDtypeStruct((5 * G, G, BB), f32),
        in_specs=[smem, smem, smem, anywhere, anywhere],
        out_specs=vmem,
        scratch_shapes=[
            pltpu.VMEM((R // 8, K, B // 2 + 1, 8, LANES), f32),
            pltpu.VMEM((R // 8 + 2, B // 2 + 1, 8, LANES), f32),
            pltpu.VMEM((R + 2 * H, B + 8, LANES), f32),
            pltpu.VMEM((R + 2 * H, 2 * B, LANES), bf16),
            pltpu.VMEM((R + 2 * H, 8, LANES), jnp.int32),
            pltpu.VMEM((slots, 8, LANES), jnp.int32),
            pltpu.VMEM((K, B + 8, LANES), f32),
            pltpu.VMEM((K, B // 8, 8, LANES), f32),
            pltpu.VMEM((R, B, WIDE), bf16),
            pltpu.VMEM((R, B, 2 * GW), f32),
            pltpu.VMEM((H, B, 2 * GW), f32),
            pltpu.VMEM((H, B, 2 * GW), f32),
            pltpu.VMEM((R + 2 * H, 2 * B, 2 * GW), bf16),
            pltpu.VMEM((4, 2, CHUNK, 3 * GW), bf16),
            part, part, part,
            piece, piece, piece, piece, piece, piece,
            pltpu.VMEM((2, H, 8, LANES), jnp.int32),
            pltpu.VMEM((slots, PIECES, 2, B, LANES), f32),
            pltpu.VMEM((slots, PIECES, 2, B, LANES), f32),
            pltpu.VMEM((slots, 8, LANES), jnp.int32),
            pltpu.VMEM((G, 2, B + 8, LANES), f32),
            pltpu.VMEM((4 * G * B, LANES), f32),
            dma((1 + R // 8,)),
            dma((4,)), dma((4,)),
            dma((2,)), dma((2,)),
            dma((2, 3)), dma((2, 3)),
            dma((slots,)), dma((slots,)),
            dma((PIECES, slots)), dma((PIECES, slots)),
        ],
        compiler_params=pltpu.CompilerParams(
            collective_id=0, has_side_effects=True, vmem_limit_bytes=48 << 20
        ),
        name="coarse",
    )(columns.T, aggregate, owner, a_tiled, t_tiled)


def local(a_blocks, columns, tentative, aggregate, owner):
    slots = lax.axis_size("col")
    result = coarse_rows(columns, aggregate, owner, a_blocks, tentative, slots)
    return result.transpose(1, 0, 2)


def solution(mesh):
    placed = (
        P(("row", "col"), None, None),
        P(("row", "col"), None),
        P(("row", "col"), None),
        P(("row", "col")),
        P(("row", "col")),
    )
    return jax.shard_map(
        local, mesh=mesh, in_specs=placed, out_specs=P(("row", "col"), None, None), check_vma=False
    )
```

```python
import functools

import jax
import jax.numpy as jnp
from jax import lax
from jax.experimental import pallas as pl
from jax.experimental.pallas import tpu as pltpu
from jax.sharding import PartitionSpec as P

B = 64
K = 6
G = 4
R = 32
H = 8
BB = B * B
GW = G * B
LANES = 128
WIDE = K // 2 * 3 * LANES
relaxation = 2.0 / 3.0
f32 = jnp.float32
bf16 = jnp.bfloat16


def lane_low(rows):
    return lax.broadcasted_iota(jnp.int32, (rows, LANES), 1) < B


def natural_dup(half_rows, scratch):
    low = lane_low(B // 2)
    swapped = pltpu.roll(half_rows, B, 1)
    scratch[pl.ds(0, B // 2, stride=2), :] = jnp.where(low, half_rows, swapped)
    scratch[pl.ds(1, B // 2, stride=2), :] = jnp.where(low, swapped, half_rows)


MESH = pl.DeviceIdType.MESH
PIECES = 5
ROWS = 4
CHUNK = ROWS * B


def split(value):
    high = value.astype(bf16)
    return high, (value - high.astype(f32)).astype(bf16)


def coarse_kernel(
    slots, columns, aggregate, owner, a_hbm, t_hbm, out_ref,
    a_tiles, t_tiles, t_nat, t_split, labels, codes, nat, smooth, aa, p_own,
    p_low, p_high, p_split, ap, own, below_out, above_out,
    lower_0, lower_1, lower_2, upper_0, upper_1, upper_2, label_rims, send, recv, got, chosen, pairs,
    load_sem, rim_send, rim_recv, halo_send, halo_recv, near_send, near_recv, code_send, code_recv, row_send, row_recv,
):
    me, row = lax.axis_index("col"), lax.axis_index("row")
    rows = lax.axis_size("row")
    device, count = row * slots + me, rows * slots

    def place(index):
        return (index // slots, lax.rem(index, slots))

    behind = place(lax.rem(device + count - 1, count))
    ahead = place(lax.rem(device + 1, count))
    lower, upper = (lower_0, lower_1, lower_2), (upper_0, upper_1, upper_2)
    core = lax.rem(me, 2)
    chip = me - core
    far, before, after = (lax.rem(chip + d, slots) for d in (4, 6, 2))
    peers = [far + core, far + 1 - core, after + core, before + core]
    peers += [after + 1 - core, before + 1 - core, chip + 1 - core]

    def load(source, target, index):
        copy = pltpu.make_async_copy(source, target, load_sem.at[index])
        copy.start()
        return copy

    half = pl.ds(0, B // 2)
    t_load = load(t_hbm, t_tiles.at[pl.ds(1, R // 8), half], 0)
    order = (0, 3, 1, 2)
    a_load = {tile: load(a_hbm.at[:, tile], a_tiles.at[tile, :, half], 1 + tile) for tile in order}
    for n in range(R):
        labels[n + H] = jnp.full((8, LANES), aggregate[n], jnp.int32)

    def here(target, i):
        return (lax.rem(lax.div(owner[i], G), slots) == target).astype(jnp.int32)

    for target in range(slots):
        code = sum(here(target, i) * (lax.rem(owner[i], G) + 1) for i in range(G))
        codes[target] = jnp.full((8, LANES), code, jnp.int32)
    barrier = pltpu.get_barrier_semaphore()
    targets = [(row, peer) for peer in peers] + [behind, ahead]
    for target in targets:
        pl.semaphore_signal(barrier, inc=1, device_id=target, device_id_type=MESH)
    pl.semaphore_wait(barrier, len(targets))

    def remote(source, target, here, there, where):
        copy = pltpu.make_async_remote_copy(
            src_ref=source, dst_ref=target, send_sem=here, recv_sem=there,
            device_id=where, device_id_type=MESH,
        )
        copy.start()
        return copy

    rims = [
        remote(t_hbm.at[R // 8 - 1], t_tiles.at[0, half], rim_send.at[0], rim_recv.at[0], ahead),
        remote(t_hbm.at[0], t_tiles.at[R // 8 + 1, half], rim_send.at[1], rim_recv.at[1], behind),
        remote(
            labels.at[pl.ds(R, H)], label_rims.at[0], rim_send.at[2], rim_recv.at[2], ahead
        ),
        remote(
            labels.at[pl.ds(H, H)], label_rims.at[1], rim_send.at[3], rim_recv.at[3],
            behind,
        ),
    ]
    copies = []
    for s, peer in enumerate(peers):
        copies.append(
            remote(codes.at[peer], got.at[me], code_send.at[s], code_recv.at[s], (row, peer))
        )
    has_low = (device > 0).astype(f32)
    has_high = (device < count - 1).astype(f32)

    low = lane_low(B)
    sub = lax.broadcasted_iota(jnp.int32, (B, LANES), 0)
    lane = lax.broadcasted_iota(jnp.int32, (B, LANES), 1)
    on_diagonal = sub == lane
    second = (lax.broadcasted_iota(jnp.int32, (8, LANES), 1) >= B).astype(jnp.int32)

    def split_basis(chunk):
        tiles = t_tiles.at[chunk].reshape((B // 2 + 1) * 8, LANES)

        def one(j, carry):
            n = chunk * 8 + j
            natural_dup(tiles[pl.ds(j, B // 2, stride=8), :], t_nat.at[n])
            high, rest = split(t_nat[n, 0:B, :])
            t_split[n, 0:B, :] = high
            t_split[n, B : 2 * B, :] = rest
            return carry

        lax.fori_loop(0, 8, one, 0, unroll=4)

    def column(n, k):
        return jnp.clip(columns[k, n] - device * R + H, 0, R + 2 * H - 1)

    def smooth_rows(tile, first=0, count=8):
        def one(r, carry):
            n = tile * 8 + r
            scale, previous, masks = None, None, []
            for k in range(K):
                ci = column(n, k)
                tiles = a_tiles.at[tile, k].reshape((B // 2 + 1) * 8, LANES)
                natural_dup(tiles[pl.ds(r, B // 2, stride=8), :], nat.at[k])
                value = nat[k, 0:B, :]
                if k == 0:
                    diagonal = jnp.sum(jnp.where(on_diagonal, value, 0.0), axis=1, keepdims=True)
                    scale = relaxation / diagonal
                high = value.astype(bf16).astype(f32)
                pieces = jnp.where(low, high, value - high).astype(bf16)
                base = (k // 2) * 3 * LANES
                aa[n, :, base + (k % 2) * LANES : base + (k % 2 + 1) * LANES] = pieces
                if k % 2 == 1:
                    both = jnp.where(low, previous, high).astype(bf16)
                    aa[n, :, base + 2 * LANES : base + 3 * LANES] = both
                previous = high
                basis = t_split[ci]
                weights = jnp.concatenate([basis[:B], basis[:B], basis[B:], basis[B:]], axis=0)
                applied = jnp.dot(
                    jnp.concatenate([pieces, pieces], axis=1), weights, preferred_element_type=f32
                )
                result = -applied * scale
                if k == 0:
                    result = result + t_nat[n + H, 0:B, :]
                smooth[k] = result.reshape(B // 8, 8, LANES)
                outside = jnp.logical_or(ci < H, ci >= R + H).astype(jnp.int32)
                masks.append(labels[ci] + outside * G)
            for part in range(4):
                total = None
                for k in range(K):
                    keep = masks[k] == 2 * part + second
                    term = jnp.where(keep[None], smooth[k], 0.0)
                    total = term if total is None else total + term
                p_own[n, :, part * LANES : (part + 1) * LANES] = total.reshape(B, LANES)
            return carry

        lax.fori_loop(first, first + count, one, 0, unroll=2)

    t_load.wait()
    for chunk in range(1, R // 8 + 1):
        split_basis(chunk)
    for copy in rims:
        copy.wait_recv()
    labels[0:H] = label_rims[0]
    labels[R + H : R + 2 * H] = label_rims[1]
    split_basis(0)
    split_basis(R // 8 + 1)
    a_load[0].wait()
    a_load[3].wait()
    halo_from_ahead, halo_from_behind = [], []
    for part in range(2):
        window = pl.ds(part * ROWS, ROWS)
        smooth_rows(0, part * ROWS, ROWS)
        halo_from_ahead.append(
            remote(
                p_own.at[window], p_high.at[window], halo_send.at[1, part],
                halo_recv.at[1, part], behind,
            )
        )
        smooth_rows(3, part * ROWS, ROWS)
        halo_from_behind.append(
            remote(
                p_own.at[pl.ds(R - H + part * ROWS, ROWS)], p_low.at[window],
                halo_send.at[0, part], halo_recv.at[0, part], ahead,
            )
        )
    for tile in (1, 2):
        a_load[tile].wait()
        smooth_rows(tile)
    halo = halo_from_ahead + halo_from_behind

    def split_own(n, carry):
        high, low = split(p_own[n])
        p_split[n + H, 0:B, :] = high
        p_split[n + H, B : 2 * B, :] = low
        return carry

    lax.fori_loop(0, R, split_own, 0, unroll=2)
    own[...] = jnp.zeros_like(own)

    def applied_rows(chunk, slot):
        for r in range(ROWS):
            n = chunk * ROWS + r
            weights, marks = [], []
            for pair in range(K // 2):
                index = [column(n, 2 * pair + t) for t in range(2)]
                basis = [p_split[ci] for ci in index]
                side = [(ci < R // 2).astype(f32) for ci in index]
                for t in range(2):
                    marks.append(jnp.full((B, LANES), side[t], f32))
                    weights.extend([basis[t][:B], basis[t][:B]])
                marks.append(jnp.where(lane_low(B), side[0], side[1]))
                weights.extend([basis[0][B:], basis[1][B:]])
            left = aa[n]
            marks = jnp.concatenate(marks, axis=1).astype(bf16)
            weights = jnp.concatenate(weights, axis=0)
            below = left * marks
            middle = jnp.dot(left, weights[:, :GW], preferred_element_type=f32)
            sides = jnp.dot(
                jnp.concatenate([below, left - below], axis=0),
                weights[:, GW:],
                preferred_element_type=f32,
            )
            for g, value in enumerate((sides[:B], middle, sides[B:])):
                high, low = split(value)
                ap[slot, 0, r * B : (r + 1) * B, g * GW : (g + 1) * GW] = high
                ap[slot, 1, r * B : (r + 1) * B, g * GW : (g + 1) * GW] = low

    def turned(chunk, part):
        block = p_own[pl.ds(chunk * ROWS, ROWS), :, part * GW : (part + 1) * GW]
        return split(block.reshape(CHUNK, GW).T)

    def product(left, slot, lanes):
        high, low = left
        value = jnp.dot(high, ap[slot, 0, :, lanes], preferred_element_type=f32)
        value = value + jnp.dot(low, ap[slot, 0, :, lanes], preferred_element_type=f32)
        return value + jnp.dot(high, ap[slot, 1, :, lanes], preferred_element_type=f32)

    def add_own(chunk, slot):
        value = product(turned(chunk, 0), slot, slice(0, 3 * GW))
        for t in range(6):
            tile = value[:, t * LANES : (t + 1) * LANES].reshape(G, B, LANES)
            own[t // 2, :, t % 2] += tile

    def inner(chunk, carry):
        applied_rows(chunk, chunk + 2)
        return carry

    lax.fori_loop(H // ROWS, (R - H) // ROWS, inner, 0)

    def take_halo(arriving, source, base):
        for copy in arriving:
            copy.wait_recv()

        def split_halo(n, carry):
            for side in range(2):
                high, rest = split(source[n, :, (1 - side) * GW : (2 - side) * GW])
                p_split[base + n, 0:B, side * GW : (side + 1) * GW] = high
                p_split[base + n, B : 2 * B, side * GW : (side + 1) * GW] = rest
            return carry

        lax.fori_loop(0, H, split_halo, 0, unroll=2)

    near = {}

    def rim(first, side, out, landing, turns, where):
        def one(index, carry):
            applied_rows(first + index, 2 * side + index)
            return carry

        lax.fori_loop(0, 2, one, 0)
        lefts = [turned(first + index, 1) for index in range(2)]
        for g in turns:
            lanes = slice(g * GW, (g + 1) * GW)
            value = product(lefts[0], 2 * side, lanes) + product(lefts[1], 2 * side + 1, lanes)
            for half in range(2):
                tile = value[:, half * LANES : (half + 1) * LANES].reshape(G, B, LANES)
                out[g, :, half] = tile
            near[side, g] = remote(
                out.at[g], landing[g], near_send.at[side, g], near_recv.at[side, g], where
            )

    take_halo(halo_from_ahead, p_high, R + H)
    rim((R - H) // ROWS, 0, above_out, lower, (0, 1, 2), ahead)
    take_halo(halo_from_behind, p_low, 0)
    rim(0, 1, below_out, upper, (2, 1, 0), behind)

    def sum_own():
        for index in range(2):
            add_own((R - H) // ROWS + index, index)
            add_own(index, 2 + index)

        def inner_own(chunk, carry):
            add_own(chunk, chunk + 2)
            return carry

        lax.fori_loop(H // ROWS, (R - H) // ROWS, inner_own, 0)

    def build(target, piece):
        a = functools.reduce(jnp.maximum, [here(target, i) * i for i in range(1, G)])
        for half in range(2):
            terms = []
            if piece < 3:
                terms.append(lower[piece][a, half] * has_low)
            if 1 <= piece < 4:
                terms.append(own[piece - 1, a, half])
            if piece >= 2:
                terms.append(upper[piece - 2][a, half] * has_high)
            send[target, piece, half] = functools.reduce(jnp.add, terms)

    needs = {0: [(0, 0)], 4: [(1, 2)], 1: [(0, 1)], 3: [(1, 1)], 2: [(0, 2), (1, 0)]}
    pieces_order = (0, 4, 1, 3, 2)
    arrivals = {}
    for step, piece in enumerate(pieces_order):
        if step == 1:
            sum_own()
        for key in needs[piece]:
            near[key].wait_recv()
        arrivals[piece] = []
        for s, peer in enumerate(peers):
            build(peer, piece)
            arrivals[piece].append(
                remote(
                    send.at[peer, piece], recv.at[me, piece],
                    row_send.at[piece, s], row_recv.at[piece, s], (row, peer),
                )
            )
        build(me, piece)

    for copy in copies:
        copy.wait_recv()
    half_low = lane_low(B // 2)
    for piece in pieces_order:
        for copy in arrivals[piece]:
            copy.wait_recv()
        for half in range(2):
            totals = [None] * G
            for index in range(slots):
                if index == slots - 1:
                    code, block = codes[me], send[me, piece, half]
                else:
                    code, block = got[peers[index]], recv[peers[index], piece, half]
                block = block.reshape(B // 8, 8, LANES)
                for g in range(G):
                    term = jnp.where((code == g + 1)[None], block, 0.0)
                    totals[g] = term if totals[g] is None else totals[g] + term
            for g in range(G):
                chosen[g, half, 0:B, :] = totals[g].reshape(B, LANES)
        for g in range(G):
            for half in range(2):
                even = chosen[g, half, pl.ds(0, B // 2, stride=2), :]
                odd = chosen[g, half, pl.ds(1, B // 2, stride=2), :]
                base = (g * 2 + half) * B
                pairs[base : base + B // 2, :] = jnp.where(
                    half_low, even, pltpu.roll(odd, B, 1)
                )
                pairs[base + B // 2 : base + B, :] = jnp.where(
                    half_low, pltpu.roll(even, B, 1), odd
                )

        def write(c, carry, piece=piece):
            lanes = pl.ds(pl.multiple_of(c * LANES, LANES), LANES)
            for col in range(4):
                rows_of = pl.ds(col * (B // 2) + c, G, stride=2 * B)
                out_ref[piece * 4 + col, :, lanes] = pairs[rows_of, :]
            return carry

        lax.fori_loop(0, B // 2, write, 0, unroll=4)
    for copy in rims + halo + list(near.values()) + copies:
        copy.wait_send()
    for piece in pieces_order:
        for copy in arrivals[piece]:
            copy.wait_send()


def coarse_rows(columns, aggregate, owner, a_blocks, tentative, slots):
    hbm = pl.BlockSpec(memory_space=pltpu.HBM)
    vmem = pl.BlockSpec(memory_space=pltpu.VMEM)
    smem = pl.BlockSpec(memory_space=pltpu.SMEM)
    dma = pltpu.SemaphoreType.DMA
    part = pltpu.VMEM((3, G, 2, B, LANES), f32)
    piece = pltpu.VMEM((G, 2, B, LANES), f32)
    a_tiled = a_blocks.reshape(R // 8, 8, K, B // 2, LANES).transpose(2, 0, 3, 1, 4)
    t_tiled = tentative.reshape(R // 8, 8, B // 2, LANES).transpose(0, 2, 1, 3)
    return pl.pallas_call(
        functools.partial(coarse_kernel, slots),
        out_shape=jax.ShapeDtypeStruct((5 * G, G, BB), f32),
        in_specs=[smem, smem, smem, hbm, hbm],
        out_specs=vmem,
        scratch_shapes=[
            pltpu.VMEM((R // 8, K, B // 2 + 1, 8, LANES), f32),
            pltpu.VMEM((R // 8 + 2, B // 2 + 1, 8, LANES), f32),
            pltpu.VMEM((R + 2 * H, B + 8, LANES), f32),
            pltpu.VMEM((R + 2 * H, 2 * B, LANES), bf16),
            pltpu.VMEM((R + 2 * H, 8, LANES), jnp.int32),
            pltpu.VMEM((slots, 8, LANES), jnp.int32),
            pltpu.VMEM((K, B + 8, LANES), f32),
            pltpu.VMEM((K, B // 8, 8, LANES), f32),
            pltpu.VMEM((R, B, WIDE), bf16),
            pltpu.VMEM((R, B, 2 * GW), f32),
            pltpu.VMEM((H, B, 2 * GW), f32),
            pltpu.VMEM((H, B, 2 * GW), f32),
            pltpu.VMEM((R + 2 * H, 2 * B, 2 * GW), bf16),
            pltpu.VMEM((R // ROWS, 2, CHUNK, 3 * GW), bf16),
            part, part, part,
            piece, piece, piece, piece, piece, piece,
            pltpu.VMEM((2, H, 8, LANES), jnp.int32),
            pltpu.VMEM((slots, PIECES, 2, B, LANES), f32),
            pltpu.VMEM((slots, PIECES, 2, B, LANES), f32),
            pltpu.VMEM((slots, 8, LANES), jnp.int32),
            pltpu.VMEM((G, 2, B + 8, LANES), f32),
            pltpu.VMEM((4 * G * B, LANES), f32),
            dma((1 + R // 8,)),
            dma((4,)), dma((4,)),
            dma((2, 2)), dma((2, 2)),
            dma((2, 3)), dma((2, 3)),
            dma((slots,)), dma((slots,)),
            dma((PIECES, slots)), dma((PIECES, slots)),
        ],
        compiler_params=pltpu.CompilerParams(
            collective_id=0, has_side_effects=True, vmem_limit_bytes=62 << 20
        ),
        name="coarse",
    )(columns.T, aggregate, owner, a_tiled, t_tiled)


def local(a_blocks, columns, tentative, aggregate, owner):
    slots = lax.axis_size("col")
    result = coarse_rows(columns, aggregate, owner, a_blocks, tentative, slots)
    return result.transpose(1, 0, 2)


def solution(mesh):
    placed = (
        P(("row", "col"), None, None),
        P(("row", "col"), None),
        P(("row", "col"), None),
        P(("row", "col")),
        P(("row", "col")),
    )
    return jax.shard_map(
        local, mesh=mesh, in_specs=placed, out_specs=P(("row", "col"), None, None), check_vma=False
    )
```
